256 devices in a mesh: mem: 16 (over y, x), space: 16 (over z, core).
Axes of the slice: x: 4, y: 4, z: 8, core: 2. Of those that a mesh axis runs over, the one named last changes fastest.
Arguments:
- ensemble: bfloat16 [64, 16, 184320], P('mem', None, 'space'), may hold values from -100 to 100
- cotangent: bfloat16 [64, 16, 184320], P('mem', None, 'space'), may hold values from -6 to 6
- w_query: bfloat16 [16, 16], replicated, may hold values from -2 to 2
- w_key: bfloat16 [16, 16], replicated, may hold values from -2 to 2
- w_value: bfloat16 [16, 16], replicated, may hold values from -1.5 to 1.5
- w_out: bfloat16 [16, 16], replicated, may hold values from -1.5 to 1.5
Outputs:
- updated: float32 [64, 16, 184320], P('mem', None, 'space')
- ensemble_grad: float32 [64, 16, 184320], P('mem', None, 'space')
The draws below stay inside these ranges and needn't reach their ends.
All inputs are finite; a program needn't handle non-finite values.
Results may differ from the reference program's by a relative error of at most 0.0044.
Values may be sent and summed in bfloat16 or wider, within the bound.
A program may use at most 128 MiB of HBM per device.

```python
import math
import jax
import jax.numpy as jnp
from jax import lax

CH = 16
NLON = 1440
LAT_DEV = 8
MEMBERS = 64
NLAT = 128
CELLS = 184320
N_SPACE = 16


def weight_pair(key):
    shared = jax.random.normal(jax.random.fold_in(key, 101), (CH, CH), jnp.float32) / math.sqrt(CH)
    partner = jax.random.normal(jax.random.fold_in(key, 102), (CH, CH), jnp.float32) / math.sqrt(CH)
    return (shared, partner)


def key_matrix(key):
    shared, partner = weight_pair(key)
    blended = 0.4 * shared + 0.9 * partner
    return blended


def value_pair(key):
    value_w = jnp.clip(jax.random.normal(jax.random.fold_in(key, 103), (CH, CH), jnp.float32), -6.0, 6.0) / math.sqrt(CH)
    out_w = jnp.clip(jax.random.normal(jax.random.fold_in(key, 104), (CH, CH), jnp.float32), -6.0, 6.0) / math.sqrt(CH)
    return (value_w, out_w)


def draw_w_query(key, part):
    shared, partner = weight_pair(key)
    return shared.astype(jnp.bfloat16)


def draw_w_key(key, part):
    return key_matrix(key).astype(jnp.bfloat16)


def draw_w_value(key, part):
    value_w, out_w = value_pair(key)
    return value_w.astype(jnp.bfloat16)


def draw_w_out(key, part):
    value_w, out_w = value_pair(key)
    return out_w.astype(jnp.bfloat16)


def ensemble_field(key):
    regions = NLAT // LAT_DEV
    noise = jax.random.normal(jax.random.fold_in(key, 1), (MEMBERS, CH, NLAT, NLON), jnp.float32)
    common = jax.random.normal(jax.random.fold_in(key, 2), (MEMBERS, MEMBERS), jnp.float32) / math.sqrt(MEMBERS)
    regional = jax.random.normal(jax.random.fold_in(key, 3), (regions, MEMBERS, MEMBERS), jnp.float32) / math.sqrt(MEMBERS)
    mixing = 0.25 * jnp.eye(MEMBERS, dtype=jnp.float32)[None] + 0.5 * common[None] + 0.9 * regional
    row_mixing = jnp.repeat(mixing, LAT_DEV, axis=0)
    latitude = jnp.arange(NLAT, dtype=jnp.float32) / max(NLAT - 1, 1)
    rising = 1.0 + 0.8 * latitude
    field = jnp.einsum('lmk,kcln->mcln', row_mixing, noise) * rising[None, None, :, None]
    return jnp.clip(field, -100.0, 100.0)


def draw_ensemble(key, part):
    field = ensemble_field(key)
    return field.reshape(MEMBERS, CH, NLAT * NLON).astype(jnp.bfloat16)


def draw_cotangent(key, part):
    field = ensemble_field(key)
    value_w, out_w = value_pair(key)
    mixer = jnp.dot(out_w.astype(jnp.bfloat16).astype(jnp.float32), value_w.astype(jnp.bfloat16).astype(jnp.float32), precision=lax.Precision.HIGHEST)
    echo = jnp.einsum('cd,mdln->mcln', mixer, field)
    noise = jax.random.normal(jax.random.fold_in(key, 6), (MEMBERS, CH, NLAT, NLON), jnp.float32)
    result = jnp.clip(noise + 0.2 * (field + echo), -6.0, 6.0)
    return result.reshape(MEMBERS, CH, NLAT * NLON).astype(jnp.bfloat16)


def setup_inputs(seed: int = 0) -> dict:
    streams_of = jax.random.split(jax.random.key(seed), 7)
    ensemble = draw_ensemble(jax.random.fold_in(streams_of[6], 71), 0)
    cotangent = draw_cotangent(jax.random.fold_in(streams_of[6], 71), 0)
    w_query = draw_w_query(jax.random.fold_in(streams_of[6], 71), 0)
    w_key = draw_w_key(jax.random.fold_in(streams_of[6], 71), 0)
    w_value = draw_w_value(jax.random.fold_in(streams_of[6], 71), 0)
    w_out = draw_w_out(jax.random.fold_in(streams_of[6], 71), 0)
    return dict(ensemble=ensemble, cotangent=cotangent, w_query=w_query, w_key=w_key, w_value=w_value, w_out=w_out)


def project(weight, field):
    return jnp.einsum('cd,mdp->mcp', weight.astype(jnp.float32), field.astype(jnp.float32))

def project_back(weight, field):
    return jnp.einsum('cd,mcp->mdp', weight.astype(jnp.float32), field.astype(jnp.float32))

def flatten(field):
    return field.reshape(field.shape[0], field.shape[1] * field.shape[2])

def pair_sum(left, right):
    return lax.dot_general(flatten(left), flatten(right), (((1,), (1,)), ((), ())), preferred_element_type=jnp.float32)

def normalize(scores):
    row_peak = lax.optimization_barrier(jnp.max(scores, axis=1, keepdims=True))
    exponent = jnp.exp(scores - row_peak)
    return exponent / lax.optimization_barrier(jnp.sum(exponent, axis=1, keepdims=True))

def combine(weights_half, field):
    mixed = jnp.dot(weights_half, flatten(field), preferred_element_type=jnp.float32)
    return mixed.astype(jnp.bfloat16).reshape(field.shape)

def reference(ensemble, cotangent, w_query, w_key, w_value, w_out):
    band = LAT_DEV * NLON

    def block(field, index):
        start = (index * band).astype(jnp.int32)
        return lax.dynamic_slice_in_dim(field, start, band, 2)

    def projections(index):
        piece = block(ensemble, index)
        grad_piece = block(cotangent, index)
        queries = project(w_query, piece).astype(jnp.bfloat16)
        key_field = project(w_key, piece).astype(jnp.bfloat16)
        value_field = project(w_value, piece).astype(jnp.bfloat16)
        grad_mixed = project_back(w_out, grad_piece).astype(jnp.bfloat16)
        return (piece, grad_piece, queries, key_field, value_field, grad_mixed)

    def gather_sums(index, carry):
        outcome = projections(index)
        return (carry[0] + pair_sum(outcome[2], outcome[3]), carry[1] + pair_sum(outcome[5], outcome[4]))
    zeros_pair = jnp.zeros((MEMBERS, MEMBERS), jnp.float32)
    total_scores, total_pairs = lax.fori_loop(0, N_SPACE, gather_sums, (zeros_pair, zeros_pair))
    score_scale = 1.0 / (CELLS * math.sqrt(CH))
    weights = normalize(score_scale * total_scores)
    weights_half = weights.astype(jnp.bfloat16)
    grad_scores = weights * (total_pairs - lax.optimization_barrier(jnp.sum(weights * total_pairs, axis=1, keepdims=True)))
    grad_scaled = (score_scale * grad_scores).astype(jnp.bfloat16)

    def finish(index, carry):
        updated, ensemble_grad = carry
        piece, grad_piece, queries, key_field, value_field, grad_mixed = projections(index)
        mixed = combine(weights_half, value_field)
        branch = project(w_out, mixed).astype(jnp.bfloat16)
        grad_queries = combine(grad_scaled, key_field)
        grad_keys = combine(grad_scaled.T, queries)
        grad_values = combine(weights_half.T, grad_mixed)
        grad_branch = (project_back(w_query, grad_queries) + project_back(w_key, grad_keys) + project_back(w_value, grad_values)).astype(jnp.bfloat16)
        out_block = piece.astype(jnp.float32) + branch.astype(jnp.float32)
        grad_block = grad_piece.astype(jnp.float32) + grad_branch.astype(jnp.float32)
        start = (index * band).astype(jnp.int32)
        updated = lax.dynamic_update_slice_in_dim(updated, out_block, start, 2)
        ensemble_grad = lax.dynamic_update_slice_in_dim(ensemble_grad, grad_block, start, 2)
        return (updated, ensemble_grad)
    empty = jnp.zeros((MEMBERS, CH, CELLS), jnp.float32)
    updated, ensemble_grad = lax.fori_loop(0, N_SPACE, finish, (empty, empty))
    return (updated, ensemble_grad)
```

```python
import functools
import math

import jax
import jax.numpy as jnp
from jax import lax
from jax.experimental import pallas as pl
from jax.experimental.pallas import tpu as pltpu
from jax.sharding import Mesh
from jax.sharding import PartitionSpec as P

MESH = pl.DeviceIdType.MESH
F32 = jnp.float32
BF16 = jnp.bfloat16
HIGH = lax.Precision.HIGHEST

NX, NY, NZ, NC = 4, 4, 8, 2
PEERS = NX * NY
CH = 16
MEM_DEV = 4
ROWS = MEM_DEV * CH
MEMBERS = MEM_DEV * PEERS
ALL = ROWS * PEERS
TILE = 128
MAIN = 5
EXTRA = 10
WIDTH = (MAIN + 1) * TILE
CELL_DEV = 11520
CHUNKS = ((0, 256), (256, 256), (512, 128))
XLO = MAIN * TILE
HOPS = (1, 3, 2)


def nt(a, b, precision=None):
    return lax.dot_general(
        a, b, (((1,), (1,)), ((), ())), precision=precision, preferred_element_type=F32
    )


def tn(a, b, precision=None):
    return lax.dot_general(
        a, b, (((0,), (0,)), ((), ())), precision=precision, preferred_element_type=F32
    )


def hop(i):
    return 2 - i + 3 * (i // 2) + 2 * (i // 3)


def kernel(
    scale,
    e_hbm,
    c_hbm,
    wq_ref,
    wk_ref,
    wv_ref,
    wo_ref,
    ob,
    og,
    re1,
    rc1,
    e_all,
    c_all,
    bm,
    gm,
    rb,
    rg,
    sacc,
    pacc,
    consts,
    sfull,
    cbuf,
    ysrc,
    ybuf,
    xsrc,
    xbuf,
    zsrc,
    zbuf,
    sfin,
    wexp,
    wtexp,
    gexp,
    gtexp,
    dblk,
    gblk,
    tblk,
    s1_send,
    s1_recv,
    s1x_send,
    s1x_recv,
    s2_send,
    s2_recv,
    s2x_send,
    s2x_recv,
    c_sem,
    y_sem,
    x_sem,
    z_sem,
    f_sem,
    q1_send,
    q1_recv,
    q1x_send,
    q1x_recv,
    q2_send,
    q2x_send,
    o_recv,
):
    y, x = lax.axis_index("y"), lax.axis_index("x")
    z, c = lax.axis_index("z"), lax.axis_index("c")

    def at(dy=0, dx=0, dz=0, dc=0):
        return (
            lax.rem(y + dy, NY),
            lax.rem(x + dx, NX),
            lax.rem(z + dz, NZ),
            lax.rem(c + dc, NC),
        )

    def order(yd, xd):
        return 4 * lax.rem(xd + yd + 2 * c, 4) + yd

    def lanes(yd, xd, lo, width):
        return pl.ds(pl.multiple_of((4 * yd + xd) * XLO + lo, TILE), width)

    def extra_lanes(yd, xd):
        return pl.ds(pl.multiple_of((MAIN * PEERS + order(yd, xd)) * TILE, TILE), TILE)

    def remote(src, dst, send, recv, device):
        pltpu.make_async_remote_copy(
            src_ref=src, dst_ref=dst, send_sem=send, recv_sem=recv, device_id=device, device_id_type=MESH
        ).start()

    def local(src, dst, sem):
        pltpu.make_async_copy(src, dst, sem).start()

    def await_bytes(view, sem):
        pltpu.make_async_copy(view, view, sem).wait()

    barrier = pltpu.get_barrier_semaphore()
    partners = [at(dc=1)]
    partners += [at(dy=d) for d in (1, 2, 3)] + [at(dx=d) for d in (1, 2, 3)]
    partners += [at(dz=d) for d in range(1, NZ)]
    for device in partners:
        pl.semaphore_signal(barrier, inc=1, device_id=device, device_id_type=MESH)
    pl.semaphore_wait(barrier, len(partners))

    for j, (lo, width) in enumerate(CHUNKS):
        for d in HOPS:

            @pl.loop(0, 4)
            def _(k, j=j, lo=lo, width=width, d=d):
                xd, yd = lax.rem(x + d, 4), lax.rem(y + d, 4)
                part = pl.ds(lo, width)
                remote(
                    e_hbm.at[:, lanes(k, xd, lo, width)],
                    re1.at[k, x, :, part],
                    s1_send.at[0],
                    s1_recv.at[0, j],
                    at(dx=d),
                )
                remote(
                    c_hbm.at[:, lanes(yd, k, lo, width)],
                    rc1.at[k, y, :, part],
                    s1_send.at[1],
                    s1_recv.at[1, j],
                    at(dy=d),
                )

        @pl.loop(0, 4)
        def _(k, j=j, lo=lo, width=width):
            part = pl.ds(lo, width)
            local(e_hbm.at[:, lanes(k, x, lo, width)], re1.at[k, x, :, part], s1_recv.at[0, j])
            local(c_hbm.at[:, lanes(y, k, lo, width)], rc1.at[k, y, :, part], s1_recv.at[1, j])

    last = pl.ds(XLO, TILE)
    for d in HOPS:

        @pl.loop(0, 4)
        def _(k, d=d):
            xd, yd = lax.rem(x + d, 4), lax.rem(y + d, 4)

            @pl.when(order(k, xd) < EXTRA)
            def _():
                remote(
                    e_hbm.at[:, extra_lanes(k, xd)],
                    re1.at[k, x, :, last],
                    s1x_send.at[0, d, k],
                    s1x_recv.at[0, k],
                    at(dx=d),
                )

            @pl.when(order(yd, k) < EXTRA)
            def _():
                remote(
                    c_hbm.at[:, extra_lanes(yd, k)],
                    rc1.at[k, y, :, last],
                    s1x_send.at[1, d, k],
                    s1x_recv.at[1, k],
                    at(dy=d),
                )

    @pl.loop(0, 4)
    def _(k):
        @pl.when(order(k, x) < EXTRA)
        def _():
            local(e_hbm.at[:, extra_lanes(k, x)], re1.at[k, x, :, last], s1x_recv.at[0, k])

        @pl.when(order(y, k) < EXTRA)
        def _():
            local(c_hbm.at[:, extra_lanes(y, k)], rc1.at[k, y, :, last], s1x_recv.at[1, k])

    @pl.when(order(y, x) >= EXTRA)
    def _():
        e_all[:, :, :, XLO:] = jnp.zeros((4, 4, ROWS, TILE), BF16)
        c_all[:, :, :, XLO:] = jnp.zeros((4, 4, ROWS, TILE), BF16)

    sacc[...] = jnp.zeros_like(sacc)
    pacc[...] = jnp.zeros_like(pacc)
    a_mat = tn(wq_ref[...], wk_ref[...])
    at_mat = tn(wk_ref[...], wq_ref[...])
    m_mat = jnp.dot(wo_ref[...], wv_ref[...], preferred_element_type=F32)
    mt_mat = lax.dot_general(
        wv_ref[...], wo_ref[...], (((0,), (1,)), ((), ())), preferred_element_type=F32
    )
    row16 = lax.broadcasted_iota(jnp.int32, (CH, 256), 0)
    lane16 = lax.rem(lax.broadcasted_iota(jnp.int32, (CH, 256), 1), CH)
    repeat = (row16 == lane16).astype(F32)
    for i, mat in enumerate((a_mat, at_mat, m_mat, mt_mat)):
        consts[i] = jnp.dot(mat, repeat, precision=HIGH, preferred_element_type=F32)

    for j, (lo, width) in enumerate(CHUNKS):
        part = pl.ds(lo, width)
        await_bytes(re1.at[:, :, :, part], s1_recv.at[0, j])
        await_bytes(rc1.at[:, :, :, part], s1_recv.at[1, j])
        for d in HOPS:
            yd, xd = lax.rem(y + d, 4), lax.rem(x + d, 4)
            remote(re1.at[yd, :, :, part], e_all.at[y, :, :, part], s2_send.at[0], s2_recv.at[0, j], at(dy=d))
            remote(rc1.at[xd, :, :, part], c_all.at[:, x, :, part], s2_send.at[1], s2_recv.at[1, j], at(dx=d))
        local(re1.at[y, :, :, part], e_all.at[y, :, :, part], s2_recv.at[0, j])
        local(rc1.at[x, :, :, part], c_all.at[:, x, :, part], s2_recv.at[1, j])

    for k in range(4):

        @pl.when(order(k, x) < EXTRA)
        def _(k=k):
            await_bytes(re1.at[k, :, :, last], s1x_recv.at[0, k])

        @pl.when(order(y, k) < EXTRA)
        def _(k=k):
            await_bytes(rc1.at[k, :, :, last], s1x_recv.at[1, k])

    for d in HOPS:
        yd, xd = lax.rem(y + d, 4), lax.rem(x + d, 4)

        @pl.when(order(yd, x) < EXTRA)
        def _(d=d, yd=yd):
            remote(re1.at[yd, :, :, last], e_all.at[y, :, :, last], s2x_send.at[0, d], s2x_recv.at[0], at(dy=d))

        @pl.when(order(y, xd) < EXTRA)
        def _(d=d, xd=xd):
            remote(rc1.at[xd, :, :, last], c_all.at[:, x, :, last], s2x_send.at[1, d], s2x_recv.at[1], at(dx=d))

    mine = order(y, x) < EXTRA

    @pl.when(mine)
    def _():
        local(re1.at[y, :, :, last], e_all.at[y, :, :, last], s2x_recv.at[0])
        local(rc1.at[x, :, :, last], c_all.at[:, x, :, last], s2x_recv.at[1])

    def gram(lo):
        @pl.loop(0, 4)
        def _(r):
            rows = pl.ds(pl.multiple_of(r * CH, CH), CH)
            left_e = e_all[r, :, :, lo : lo + 256].reshape(256, 256)
            left_c = c_all[r, :, :, lo : lo + 256].reshape(256, 256)
            for q in range(4):
                right = e_all[q, :, :, lo : lo + 256].reshape(256, 256)
                cols = slice(256 * q, 256 * q + 256)
                s = nt(left_e, right).reshape(CH, CH, 256) * consts[0][None]
                sacc[rows, cols] += jnp.sum(s, axis=1)
                p = nt(left_c, right).reshape(CH, CH, 256) * consts[2][None]
                pacc[rows, cols] += jnp.sum(p, axis=1)

    for j, (lo, width) in enumerate(CHUNKS):
        part = pl.ds(lo, width)
        await_bytes(e_all.at[:, :, :, part], s2_recv.at[0, j])
        await_bytes(c_all.at[:, :, :, part], s2_recv.at[1, j])
        if j == len(CHUNKS) - 1:

            @pl.when(mine)
            def _():
                await_bytes(e_all.at[:, :, :, last], s2x_recv.at[0])
                await_bytes(c_all.at[:, :, :, last], s2x_recv.at[1])

        gram(lo)

    group = lax.broadcasted_iota(jnp.int32, (ALL, 2 * MEMBERS), 0) // CH
    column = lax.broadcasted_iota(jnp.int32, (ALL, 2 * MEMBERS), 1)
    fold_s = (group == column).astype(F32)
    fold_p = (group == column - MEMBERS).astype(F32)
    sfull[...] = jnp.dot(sacc[...], fold_s, precision=HIGH, preferred_element_type=F32) + jnp.dot(
        pacc[...], fold_p, precision=HIGH, preferred_element_type=F32
    )
    half = MEMBERS // 2
    own = pl.ds(pl.multiple_of(half * c, half), half)
    other = pl.ds(pl.multiple_of(half * (1 - c), half), half)

    def swap(src, dst, sem, device):
        return pltpu.make_async_remote_copy(
            src_ref=src,
            dst_ref=dst,
            send_sem=sem.at[0],
            recv_sem=sem.at[1],
            device_id=device,
            device_id_type=MESH,
        )

    copy = swap(sfull.at[other], cbuf, c_sem, at(dc=1))
    copy.start()
    copy.wait()
    ysrc[...] = sfull[own] + cbuf[...]
    for src, buf, sem, nxt, where in (
        (ysrc, ybuf, y_sem, xsrc, [at(dy=d) for d in (1, 2, 3)]),
        (xsrc, xbuf, x_sem, zsrc, [at(dx=d) for d in (1, 2, 3)]),
        (zsrc, zbuf, z_sem, sfin, [at(dz=d) for d in range(1, NZ)]),
    ):
        copies = [swap(src, buf.at[i], sem.at[i], device) for i, device in enumerate(where)]
        for copy in copies:
            copy.start()
        for copy in copies:
            copy.wait()
        total = src[...]
        for i in range(len(where)):
            total += buf[i]
        if nxt is sfin:
            sfin[own] = total
        else:
            nxt[...] = total
    copy = swap(sfin.at[own], sfin.at[own], f_sem, at(dc=1))
    copy.start()
    copy.wait()

    scores = scale * sfin[:, :MEMBERS]
    pairs = sfin[:, MEMBERS:]
    peak = jnp.max(scores, axis=1, keepdims=True)
    exponent = jnp.exp(scores - peak)
    weights = exponent / jnp.sum(exponent, axis=1, keepdims=True)
    grad_scores = weights * (pairs - jnp.sum(weights * pairs, axis=1, keepdims=True))
    w_half = weights.astype(BF16)
    g_half = (scale * grad_scores).astype(BF16)
    spread = (
        lax.broadcasted_iota(jnp.int32, (MEMBERS, ALL), 0)
        == lax.broadcasted_iota(jnp.int32, (MEMBERS, ALL), 1) // CH
    ).astype(BF16)
    wexp[...] = jnp.dot(w_half, spread, preferred_element_type=F32)
    gexp[...] = jnp.dot(g_half, spread, preferred_element_type=F32)
    wtexp[...] = tn(w_half, spread)
    gtexp[...] = tn(g_half, spread)

    def times(coefficients, row, const):
        line = jnp.broadcast_to(coefficients[pl.ds(row, 1), :], (CH, ALL))
        return line * jnp.concatenate([consts[const]] * 4, axis=1)

    @pl.loop(0, 4)
    def _(i):
        d = hop(i)
        yh, xh = lax.rem(y + d, 4), lax.rem(x + d, 4)

        @pl.loop(0, CH)
        def _(k):
            rows = pl.ds(pl.multiple_of(k * CH, CH), CH)
            dblk[rows, :] = times(wexp, yh * CH + k, 2).astype(BF16)

        for q in range(3):
            part = slice(256 * q, 256 * q + 256)
            right = e_all[:, :, :, part].reshape(ALL, 256)
            out = jnp.dot(dblk[...], right, preferred_element_type=F32)
            bm[yh, :, :, part] = out.astype(BF16).reshape(4, ROWS, 256)

        main = pl.ds(0, XLO)

        @pl.when(i < 3)
        def _():
            remote(
                bm.at[yh, :, :, main], rb.at[y, :, :, main], q1_send.at[0], q1_recv.at[0, y], (yh, x, z, c)
            )

            @pl.when(mine)
            def _():
                remote(
                    bm.at[yh, :, :, last], rb.at[y, :, :, last], q1x_send.at[0], q1x_recv.at[0, y], (yh, x, z, c)
                )

        @pl.when(i == 3)
        def _():
            local(bm.at[yh, :, :, main], rb.at[y, :, :, main], q1_recv.at[0, y])

            @pl.when(mine)
            def _():
                local(bm.at[yh, :, :, last], rb.at[y, :, :, last], q1x_recv.at[0, y])

        @pl.loop(0, CH)
        def _(k):
            rows = pl.ds(pl.multiple_of(k * CH, CH), CH)
            row = (k // 4) * CH + xh * 4 + lax.rem(k, 4)
            tblk[rows, :] = times(wtexp, row, 3).astype(BF16)
            gblk[rows, :] = (times(gexp, row, 0) + times(gtexp, row, 1)).astype(BF16)

        for q in range(3):
            part = slice(256 * q, 256 * q + 256)
            right = e_all[:, :, :, part].reshape(ALL, 256)
            out = jnp.dot(gblk[...], right, preferred_element_type=F32)
            right = c_all[:, :, :, part].reshape(ALL, 256)
            out += jnp.dot(tblk[...], right, preferred_element_type=F32)
            gm[xh, :, :, part] = out.astype(BF16).reshape(4, ROWS, 256)

        @pl.when(i < 3)
        def _():
            remote(
                gm.at[xh, :, :, main], rg.at[x, :, :, main], q1_send.at[1], q1_recv.at[1, x], (y, xh, z, c)
            )

            @pl.when(mine)
            def _():
                remote(
                    gm.at[xh, :, :, last], rg.at[x, :, :, last], q1x_send.at[1], q1x_recv.at[1, x], (y, xh, z, c)
                )

        @pl.when(i == 3)
        def _():
            local(gm.at[xh, :, :, main], rg.at[x, :, :, main], q1_recv.at[1, x])

            @pl.when(mine)
            def _():
                local(gm.at[xh, :, :, last], rg.at[x, :, :, last], q1x_recv.at[1, x])

    @pl.loop(0, 4)
    def _(i):
        s = lax.rem(8 - hop(i), 4)
        ys, xs = lax.rem(y + s, 4), lax.rem(x + s, 4)
        main = pl.ds(0, XLO)
        await_bytes(rb.at[ys, :, :, main], q1_recv.at[0, ys])
        await_bytes(rg.at[xs, :, :, main], q1_recv.at[1, xs])
        for d in HOPS:
            xh, yh = lax.rem(x + d, 4), lax.rem(y + d, 4)
            remote(
                rb.at[ys, xh, :, main], ob.at[:, lanes(ys, x, 0, XLO)], q2_send.at[0], o_recv.at[0], at(dx=d)
            )
            remote(
                rg.at[xs, yh, :, main], og.at[:, lanes(y, xs, 0, XLO)], q2_send.at[1], o_recv.at[1], at(dy=d)
            )
        local(rb.at[ys, x, :, main], ob.at[:, lanes(ys, x, 0, XLO)], o_recv.at[0])
        local(rg.at[xs, y, :, main], og.at[:, lanes(y, xs, 0, XLO)], o_recv.at[1])

        @pl.when(order(ys, x) < EXTRA)
        def _():
            await_bytes(rb.at[ys, :, :, last], q1x_recv.at[0, ys])
            for d in HOPS:
                xh = lax.rem(x + d, 4)
                remote(
                    rb.at[ys, xh, :, last], ob.at[:, extra_lanes(ys, x)], q2x_send.at[0, ys], o_recv.at[0], at(dx=d)
                )
            local(rb.at[ys, x, :, last], ob.at[:, extra_lanes(ys, x)], o_recv.at[0])

        @pl.when(order(y, xs) < EXTRA)
        def _():
            await_bytes(rg.at[xs, :, :, last], q1x_recv.at[1, xs])
            for d in HOPS:
                yh = lax.rem(y + d, 4)
                remote(
                    rg.at[xs, yh, :, last], og.at[:, extra_lanes(y, xs)], q2x_send.at[1, xs], o_recv.at[1], at(dy=d)
                )
            local(rg.at[xs, y, :, last], og.at[:, extra_lanes(y, xs)], o_recv.at[1])

    for t in range(2):
        buf = (re1, rc1)[t]
        await_bytes(buf.at[pl.ds(0, 3), :, :, pl.ds(0, XLO)], s1_send.at[t])
        await_bytes(buf.at[pl.ds(0, 3), :, :, pl.ds(0, XLO)], s2_send.at[t])
        await_bytes(buf.at[pl.ds(0, 3), :, :, pl.ds(0, XLO)], q1_send.at[t])
        await_bytes(buf.at[pl.ds(0, 3), :, :, pl.ds(0, XLO)], q2_send.at[t])

        @pl.when(mine)
        def _(t=t, buf=buf):
            await_bytes(buf.at[pl.ds(0, 3), :, :, last], q1x_send.at[t])

    for d in HOPS:
        xd, yd = lax.rem(x + d, 4), lax.rem(y + d, 4)
        for k in range(4):

            @pl.when(order(k, xd) < EXTRA)
            def _(d=d, k=k):
                await_bytes(re1.at[k, 0, :, last], s1x_send.at[0, d, k])

            @pl.when(order(yd, k) < EXTRA)
            def _(d=d, k=k):
                await_bytes(rc1.at[k, 0, :, last], s1x_send.at[1, d, k])

        @pl.when(order(yd, x) < EXTRA)
        def _(d=d):
            await_bytes(re1.at[0, :, :, last], s2x_send.at[0, d])

        @pl.when(order(y, xd) < EXTRA)
        def _(d=d):
            await_bytes(rc1.at[0, :, :, last], s2x_send.at[1, d])

    for k in range(4):

        @pl.when(order(k, x) < EXTRA)
        def _(k=k):
            await_bytes(re1.at[0, pl.ds(0, 3), :, last], q2x_send.at[0, k])

        @pl.when(order(y, k) < EXTRA)
        def _(k=k):
            await_bytes(rc1.at[0, pl.ds(0, 3), :, last], q2x_send.at[1, k])

    await_bytes(ob, o_recv.at[0])
    await_bytes(og, o_recv.at[1])


def shards(scale, ensemble, cotangent, w_query, w_key, w_value, w_out):
    shape = ensemble.shape
    field = lambda: pltpu.VMEM((4, 4, ROWS, WIDTH), BF16)
    small = lambda *lead: pltpu.VMEM(lead + (MEMBERS // 2, 2 * MEMBERS), F32)
    dma = pltpu.SemaphoreType.DMA
    flat = jax.ShapeDtypeStruct((ROWS, CELL_DEV), BF16)
    hbm = pl.BlockSpec(memory_space=pl.ANY)
    vmem = pl.BlockSpec(memory_space=pltpu.VMEM)
    branch, grad = pl.pallas_call(
        functools.partial(kernel, scale),
        out_shape=(flat, flat),
        in_specs=[hbm, hbm, vmem, vmem, vmem, vmem],
        out_specs=(hbm, hbm),
        scratch_shapes=[field() for _ in range(8)]
        + [
            pltpu.VMEM((MEMBERS, ALL), F32),
            pltpu.VMEM((MEMBERS, ALL), F32),
            pltpu.VMEM((4, CH, 256), F32),
            pltpu.VMEM((MEMBERS, 2 * MEMBERS), F32),
            small(),
            small(),
            small(3),
            small(),
            small(3),
            small(),
            small(NZ - 1),
            pltpu.VMEM((MEMBERS, 2 * MEMBERS), F32),
        ]
        + [pltpu.VMEM((MEMBERS, ALL), F32) for _ in range(4)]
        + [pltpu.VMEM((256, ALL), BF16) for _ in range(3)]
        + [
            dma((2,)),
            dma((2, 3)),
            dma((2, 4, 4)),
            dma((2, 4)),
            dma((2,)),
            dma((2, 3)),
            dma((2, 4)),
            dma((2,)),
            dma((2,)),
            dma((3, 2)),
            dma((3, 2)),
            dma((NZ - 1, 2)),
            dma((2,)),
            dma((2,)),
            dma((2, 4)),
            dma((2,)),
            dma((2, 4)),
            dma((2,)),
            dma((2, 4)),
            dma((2,)),
        ],
        compiler_params=pltpu.CompilerParams(
            collective_id=0, has_side_effects=True, vmem_limit_bytes=48 * 2**20
        ),
    )(
        ensemble.reshape(ROWS, CELL_DEV),
        cotangent.reshape(ROWS, CELL_DEV),
        w_query,
        w_key,
        w_value,
        w_out,
    )
    updated = ensemble.astype(F32) + branch.reshape(shape).astype(F32)
    ensemble_grad = cotangent.astype(F32) + grad.reshape(shape).astype(F32)
    return updated, ensemble_grad


def solution(mesh):
    torus = Mesh(mesh.devices.reshape(NY, NX, NZ, NC), ("y", "x", "z", "c"))
    scale = 1.0 / (CELL_DEV * NZ * NC * math.sqrt(CH))
    placed = P(("y", "x"), None, ("z", "c"))
    return jax.shard_map(
        functools.partial(shards, scale),
        mesh=torus,
        in_specs=(placed, placed, P(), P(), P(), P()),
        out_specs=(placed, placed),
        check_vma=False,
    )
```

```python
import functools
import math

import jax
import jax.numpy as jnp
from jax import lax
from jax.experimental import pallas as pl
from jax.experimental.pallas import tpu as pltpu
from jax.sharding import Mesh
from jax.sharding import PartitionSpec as P

MESH = pl.DeviceIdType.MESH
F32 = jnp.float32
BF16 = jnp.bfloat16
HIGH = lax.Precision.HIGHEST

NX, NY, NZ, NC = 4, 4, 8, 2
PEERS = NX * NY
CH = 16
MEM_DEV = 4
ROWS = MEM_DEV * CH
MEMBERS = MEM_DEV * PEERS
ALL = ROWS * PEERS
TILE = 128
MAIN = 5
EXTRA = 10
WIDTH = (MAIN + 1) * TILE
CELL_DEV = 11520
SPAN = 3 * TILE
XLO = MAIN * TILE
HOPS = (1, 3, 2)


def nt(a, b, precision=None):
    return lax.dot_general(
        a, b, (((1,), (1,)), ((), ())), precision=precision, preferred_element_type=F32
    )


def tn(a, b, precision=None):
    return lax.dot_general(
        a, b, (((0,), (0,)), ((), ())), precision=precision, preferred_element_type=F32
    )


def kernel(
    scale,
    e_hbm,
    c_hbm,
    wq_hbm,
    wk_hbm,
    wv_hbm,
    wo_hbm,
    ob,
    og,
    weights_in,
    ea1,
    eb1,
    ca1,
    cb1,
    e_all,
    c_all,
    bm,
    gm,
    ba,
    bb,
    ga,
    gb,
    partial,
    dmat,
    tmat,
    gmat,
    acc,
    consts,
    fold_lo,
    fold_hi,
    packed,
    cbuf,
    ysrc,
    ybuf,
    xsrc,
    xbuf,
    zsrc,
    zbuf,
    fin,
    wsave,
    exp_a,
    exp_b,
    w_sem,
    s1_send,
    s1_recv,
    s1x_send,
    s1x_recv,
    s2_send,
    s2_recv,
    s2x_send,
    s2x_recv,
    c_sem,
    y_sem,
    x_sem,
    z_sem,
    f_sem,
    q1_send,
    q1_recv,
    q1x_send,
    q1x_recv,
    q2_send,
    q2x_send,
    o_recv,
):
    y, x = lax.axis_index("y"), lax.axis_index("x")
    z, c = lax.axis_index("z"), lax.axis_index("c")
    sources = (e_hbm, c_hbm)
    first_a, first_b = (ea1, ca1), (eb1, cb1)
    whole = (e_all, c_all)
    made = (bm, gm)
    back_a, back_b = (ba, ga), (bb, gb)
    homes = (ob, og)

    def at(dy=0, dx=0, dz=0, dc=0):
        return (
            lax.rem(y + dy, NY),
            lax.rem(x + dx, NX),
            lax.rem(z + dz, NZ),
            lax.rem(c + dc, NC),
        )

    def more(yd, xd):
        return 4 * lax.rem(xd + yd + 2 * c, 4) + yd

    def has_more(yd, xd):
        return more(yd, xd) < EXTRA

    def lanes(yd, xd, lo):
        return pl.ds(pl.multiple_of((4 * yd + xd) * XLO + lo, TILE), TILE)

    def more_lanes(yd, xd):
        return pl.ds(pl.multiple_of((MAIN * PEERS + more(yd, xd)) * TILE, TILE), TILE)

    def remote(src, dst, send, recv, device):
        pltpu.make_async_remote_copy(
            src_ref=src, dst_ref=dst, send_sem=send, recv_sem=recv, device_id=device, device_id_type=MESH
        ).start()

    def local(src, dst, sem):
        pltpu.make_async_copy(src, dst, sem).start()

    def await_bytes(view, sem):
        pltpu.make_async_copy(view, view, sem).wait()

    mine = has_more(y, x)
    tile = [pl.ds(TILE * k, TILE) for k in range(6)]

    def out1(t, j):
        src, pa, pb = sources[t], first_a[t], first_b[t]
        for d in HOPS:

            @pl.loop(0, 4)
            def _(k, d=d):
                xd, yd = lax.rem(x + d, 4), lax.rem(y + d, 4)
                remote(
                    src.at[:, lanes(k, xd, TILE * j)],
                    pa.at[k, x, :, tile[j]],
                    s1_send.at[t, 0],
                    s1_recv.at[t, 0, j],
                    at(dx=d),
                )
                if j < 2:
                    remote(
                        src.at[:, lanes(yd, k, SPAN + TILE * j)],
                        pb.at[k, y, :, tile[j]],
                        s1_send.at[t, 1],
                        s1_recv.at[t, 1, j],
                        at(dy=d),
                    )
                else:

                    @pl.when(has_more(yd, k))
                    def _():
                        remote(
                            src.at[:, more_lanes(yd, k)],
                            pb.at[k, y, :, tile[j]],
                            s1x_send.at[t, d, k],
                            s1x_recv.at[t, k],
                            at(dy=d),
                        )

        @pl.loop(0, 4)
        def _(k):
            local(src.at[:, lanes(k, x, TILE * j)], pa.at[k, x, :, tile[j]], s1_recv.at[t, 0, j])
            if j < 2:
                local(src.at[:, lanes(y, k, SPAN + TILE * j)], pb.at[k, y, :, tile[j]], s1_recv.at[t, 1, j])
            else:

                @pl.when(has_more(y, k))
                def _():
                    local(src.at[:, more_lanes(y, k)], pb.at[k, y, :, tile[j]], s1x_recv.at[t, k])

    def out2(t, j):
        pa, pb, dst = first_a[t], first_b[t], whole[t]
        await_bytes(pa.at[:, :, :, tile[j]], s1_recv.at[t, 0, j])
        for d in HOPS:
            yd = lax.rem(y + d, 4)
            remote(
                pa.at[yd, :, :, tile[j]], dst.at[y, :, :, tile[j]], s2_send.at[t, 0], s2_recv.at[t, 0, j], at(dy=d)
            )
        local(pa.at[y, :, :, tile[j]], dst.at[y, :, :, tile[j]], s2_recv.at[t, 0, j])
        if j < 2:
            await_bytes(pb.at[:, :, :, tile[j]], s1_recv.at[t, 1, j])
            for d in HOPS:
                xd = lax.rem(x + d, 4)
                remote(
                    pb.at[xd, :, :, tile[j]],
                    dst.at[:, x, :, tile[3 + j]],
                    s2_send.at[t, 1],
                    s2_recv.at[t, 1, j],
                    at(dx=d),
                )
            local(pb.at[x, :, :, tile[j]], dst.at[:, x, :, tile[3 + j]], s2_recv.at[t, 1, j])
        else:
            for d in HOPS:
                xd = lax.rem(x + d, 4)

                @pl.when(has_more(y, xd))
                def _(d=d, xd=xd):
                    await_bytes(pb.at[xd, :, :, tile[j]], s1x_recv.at[t, xd])
                    remote(
                        pb.at[xd, :, :, tile[j]],
                        dst.at[:, x, :, tile[3 + j]],
                        s2x_send.at[t, d],
                        s2x_recv.at[t],
                        at(dx=d),
                    )

            @pl.when(mine)
            def _():
                await_bytes(pb.at[x, :, :, tile[j]], s1x_recv.at[t, x])
                local(pb.at[x, :, :, tile[j]], dst.at[:, x, :, tile[3 + j]], s2x_recv.at[t])

    def arrived(t, j):
        await_bytes(whole[t].at[:, :, :, tile[j]], s2_recv.at[t, 0, j])
        if j < 2:
            await_bytes(whole[t].at[:, :, :, tile[3 + j]], s2_recv.at[t, 1, j])
        else:

            @pl.when(mine)
            def _():
                await_bytes(whole[t].at[:, :, :, tile[3 + j]], s2x_recv.at[t])

    def home1(t, j):
        src, pa, pb = made[t], back_a[t], back_b[t]
        for d in HOPS:
            yh, xh = lax.rem(y + d, 4), lax.rem(x + d, 4)
            remote(
                src.at[yh, :, :, tile[j]], pa.at[y, :, :, tile[j]], q1_send.at[t, 0], q1_recv.at[t, 0, j], at(dy=d)
            )
            if j < 2:
                remote(
                    src.at[:, xh, :, tile[3 + j]],
                    pb.at[x, :, :, tile[j]],
                    q1_send.at[t, 1],
                    q1_recv.at[t, 1, j],
                    at(dx=d),
                )
        local(src.at[y, :, :, tile[j]], pa.at[y, :, :, tile[j]], q1_recv.at[t, 0, j])
        if j < 2:
            local(src.at[:, x, :, tile[3 + j]], pb.at[x, :, :, tile[j]], q1_recv.at[t, 1, j])
        else:

            @pl.when(mine)
            def _():
                for d in HOPS:
                    xh = lax.rem(x + d, 4)
                    remote(
                        src.at[:, xh, :, tile[3 + j]],
                        pb.at[x, :, :, tile[j]],
                        q1x_send.at[t],
                        q1x_recv.at[t, x],
                        at(dx=d),
                    )
                local(src.at[:, x, :, tile[3 + j]], pb.at[x, :, :, tile[j]], q1x_recv.at[t, x])

    def home2(t, j):
        pa, pb, dst = back_a[t], back_b[t], homes[t]
        await_bytes(pa.at[:, :, :, tile[j]], q1_recv.at[t, 0, j])

        @pl.loop(0, 4)
        def _(s):
            for d in HOPS:
                remote(
                    pa.at[s, lax.rem(x + d, 4), :, tile[j]],
                    dst.at[:, lanes(s, x, TILE * j)],
                    q2_send.at[t, 0],
                    o_recv.at[t],
                    at(dx=d),
                )
            local(pa.at[s, x, :, tile[j]], dst.at[:, lanes(s, x, TILE * j)], o_recv.at[t])

        if j < 2:
            await_bytes(pb.at[:, :, :, tile[j]], q1_recv.at[t, 1, j])

        @pl.loop(0, 4)
        def _(s):
            if j < 2:
                for d in HOPS:
                    remote(
                        pb.at[s, lax.rem(y + d, 4), :, tile[j]],
                        dst.at[:, lanes(y, s, SPAN + TILE * j)],
                        q2_send.at[t, 1],
                        o_recv.at[t],
                        at(dy=d),
                    )
                local(pb.at[s, y, :, tile[j]], dst.at[:, lanes(y, s, SPAN + TILE * j)], o_recv.at[t])
            else:

                @pl.when(has_more(y, s))
                def _():
                    await_bytes(pb.at[s, :, :, tile[j]], q1x_recv.at[t, s])
                    for d in HOPS:
                        remote(
                            pb.at[s, lax.rem(y + d, 4), :, tile[j]],
                            dst.at[:, more_lanes(y, s)],
                            q2x_send.at[t, s],
                            o_recv.at[t],
                            at(dy=d),
                        )
                    local(pb.at[s, y, :, tile[j]], dst.at[:, more_lanes(y, s)], o_recv.at[t])

    def cells(t, j, r=None):
        ref = whole[t]
        if r is None:
            two = [ref[:, :, :, tile[k]].reshape(ALL, TILE) for k in (j, 3 + j)]
        else:
            two = [ref[r, :, :, tile[k]].reshape(256, TILE) for k in (j, 3 + j)]
        return jnp.concatenate(two, axis=1)

    def gram(t, j, const):
        @pl.loop(0, 4)
        def _(r):
            rows = pl.ds(pl.multiple_of(r * CH, CH), CH)
            left = cells(t, j, r)
            for q in range(4):
                cols = slice(256 * q, 256 * q + 256)
                s = nt(left, cells(0, j, q)).reshape(CH, CH, 256) * consts[const][None]
                if j == 0:
                    acc[rows, cols] = jnp.sum(s, axis=1)
                else:
                    acc[rows, cols] += jnp.sum(s, axis=1)

    half = MEMBERS // 4
    own = pl.ds(pl.multiple_of(half * c, half), half)
    other = pl.ds(pl.multiple_of(half * (1 - c), half), half)

    def pack(t):
        rest = acc[...]
        total = None
        for _ in range(3):
            part = rest.astype(BF16)
            rest = rest - part.astype(F32)
            both = jnp.dot(part[: MEMBERS // 2], fold_lo[...], preferred_element_type=F32)
            both += jnp.dot(part[MEMBERS // 2 :], fold_hi[...], preferred_element_type=F32)
            total = both if total is None else total + both
        packed[t] = total

    def swap(src, dst, send, recv, device):
        return pltpu.make_async_remote_copy(
            src_ref=src, dst_ref=dst, send_sem=send, recv_sem=recv, device_id=device, device_id_type=MESH
        )

    def run(copies):
        for copy in copies:
            copy.start()

    def collect(t, copies, src, buf, dst):
        for copy in copies:
            copy.wait()
        total = src[t]
        for i in range(len(copies)):
            total += buf[t, i]
        if dst is fin:
            fin[t, own] = total
        else:
            dst[t] = total

    def stage(t, name):
        if name == "core":
            return [swap(packed.at[t, other], cbuf.at[t], c_sem.at[t, 0], c_sem.at[t, 1], at(dc=1))]
        if name == "back":
            return [swap(fin.at[t, own], fin.at[t, own], f_sem.at[t, 0], f_sem.at[t, 1], at(dc=1))]
        src, buf, sem, key, count = {
            "y": (ysrc, ybuf, y_sem, "dy", NY),
            "x": (xsrc, xbuf, x_sem, "dx", NX),
            "z": (zsrc, zbuf, z_sem, "dz", NZ),
        }[name]
        return [
            swap(src.at[t], buf.at[t, d - 1], sem.at[t, d - 1, 0], sem.at[t, d - 1, 1], at(**{key: d}))
            for d in range(1, count)
        ]

    def reduce_begin(t, between):
        pack(t)
        core = stage(t, "core")
        run(core)
        core[0].wait()
        ysrc[t] = packed[t, own] + cbuf[t]
        along = stage(t, "y")
        run(along)
        between(1)
        collect(t, along, ysrc, ybuf, xsrc)
        along = stage(t, "x")
        run(along)
        between(2)
        collect(t, along, xsrc, xbuf, zsrc)
        run(stage(t, "z"))

    def reduce_z(t):
        collect(t, stage(t, "z"), zsrc, zbuf, fin)
        run(stage(t, "back"))

    def reduce_end(t):
        stage(t, "back")[0].wait()
        return jnp.concatenate([fin[t, :, :MEMBERS], fin[t, :, MEMBERS:]], axis=0)

    spread = (
        lax.broadcasted_iota(jnp.int32, (MEMBERS, ALL), 0)
        == lax.broadcasted_iota(jnp.int32, (MEMBERS, ALL), 1) // CH
    ).astype(BF16)

    def blocks(dst, *terms):
        @pl.loop(0, MEMBERS)
        def _(m):
            rows = pl.ds(pl.multiple_of(m * CH, CH), CH)
            for q in range(4):
                cols = slice(256 * q, 256 * q + 256)
                total = None
                for coefficient, const in terms:
                    term = jnp.broadcast_to(coefficient[pl.ds(m, 1), cols], (CH, 256)) * consts[const]
                    total = term if total is None else total + term
                dst[rows, cols] = total.astype(BF16)

    def put(t, j, r, value):
        value = value.astype(BF16)
        made[t][r, :, :, tile[j]] = value[:, :TILE].reshape(4, ROWS, TILE)
        made[t][r, :, :, tile[3 + j]] = value[:, TILE:].reshape(4, ROWS, TILE)

    barrier = pltpu.get_barrier_semaphore()
    partners = [at(dc=1)]
    partners += [at(dy=d) for d in (1, 2, 3)] + [at(dx=d) for d in (1, 2, 3)]
    partners += [at(dz=d) for d in range(1, NZ)]
    for device in partners:
        pl.semaphore_signal(barrier, inc=1, device_id=device, device_id_type=MESH)
    for i, ref in enumerate((wq_hbm, wk_hbm, wv_hbm, wo_hbm)):
        local(ref, weights_in.at[i], w_sem)
    pl.semaphore_wait(barrier, len(partners))

    for j in range(3):
        out1(0, j)

    @pl.when(jnp.logical_not(mine))
    def _():
        e_all[:, :, :, XLO:] = jnp.zeros((4, 4, ROWS, TILE), BF16)
        c_all[:, :, :, XLO:] = jnp.zeros((4, 4, ROWS, TILE), BF16)

    await_bytes(weights_in, w_sem)
    wq, wk, wv, wo = (weights_in[i] for i in range(4))
    a_mat = tn(wq, wk)
    at_mat = tn(wk, wq)
    m_mat = jnp.dot(wo, wv, preferred_element_type=F32)
    mt_mat = lax.dot_general(wv, wo, (((0,), (1,)), ((), ())), preferred_element_type=F32)
    row16 = lax.broadcasted_iota(jnp.int32, (CH, 256), 0)
    lane16 = lax.rem(lax.broadcasted_iota(jnp.int32, (CH, 256), 1), CH)
    repeat = (row16 == lane16).astype(F32)
    for i, mat in enumerate((a_mat, at_mat, m_mat, mt_mat)):
        consts[i] = jnp.dot(mat, repeat, precision=HIGH, preferred_element_type=F32)
    group = lax.broadcasted_iota(jnp.int32, (ALL, 2 * MEMBERS), 0) // CH
    column = lax.broadcasted_iota(jnp.int32, (ALL, 2 * MEMBERS), 1)
    fold_lo[...] = (group == column).astype(BF16)
    fold_hi[...] = (group == column - MEMBERS).astype(BF16)

    for j in range(3):
        out2(0, j)
    out1(1, 0)
    for j in range(3):
        arrived(0, j)
        gram(0, j, 0)

    reduce_begin(0, lambda j: out1(1, j))
    out2(1, 0)
    out2(1, 1)
    reduce_z(0)
    out2(1, 2)
    scores = scale * reduce_end(0)
    exponent = jnp.exp(scores - jnp.max(scores, axis=1, keepdims=True))
    weights = exponent / jnp.sum(exponent, axis=1, keepdims=True)
    wsave[...] = weights
    w_half = weights.astype(BF16)
    exp_a[...] = jnp.dot(w_half, spread, preferred_element_type=F32)
    blocks(dmat, (exp_a, 2))

    def mix_branch(j):
        right = cells(0, j)
        for r in range(4):
            put(0, j, r, jnp.dot(dmat[256 * r : 256 * r + 256, :], right, preferred_element_type=F32))

    mix_branch(0)
    home1(0, 0)
    mix_branch(1)
    mix_branch(2)
    for j in range(3):
        arrived(1, j)
        gram(1, j, 2)

    reduce_begin(1, lambda j: home1(0, j))
    home2(0, 0)
    exp_b[...] = tn(wsave[...].astype(BF16), spread)
    blocks(tmat, (exp_b, 3))
    for j in range(3):
        right = cells(1, j)
        for r in range(4):
            rows = slice(256 * r, 256 * r + 256)
            partial[j, rows, :] = jnp.dot(tmat[rows, :], right, preferred_element_type=F32)
    home2(0, 1)
    reduce_z(1)
    home2(0, 2)
    pairs = reduce_end(1)
    weights = wsave[...]
    grad_scores = weights * (pairs - jnp.sum(weights * pairs, axis=1, keepdims=True))
    g_half = (scale * grad_scores).astype(BF16)
    exp_a[...] = jnp.dot(g_half, spread, preferred_element_type=F32)
    exp_b[...] = tn(g_half, spread)
    blocks(gmat, (exp_a, 0), (exp_b, 1))
    for j in range(3):
        right = cells(0, j)
        for r in range(4):
            rows = slice(256 * r, 256 * r + 256)
            out = jnp.dot(gmat[rows, :], right, preferred_element_type=F32)
            put(1, j, r, out + partial[j, rows, :])
        home1(1, j)
    for j in range(3):
        home2(1, j)

    for t in range(2):
        for sem in (s1_send, s2_send, q1_send, q2_send):
            await_bytes(ea1.at[pl.ds(0, 3)], sem.at[t, 0])
            await_bytes(ea1.at[pl.ds(0, 3), :, :, pl.ds(0, 2 * TILE)], sem.at[t, 1])

        @pl.when(mine)
        def _(t=t):
            await_bytes(ea1.at[pl.ds(0, 3), :, :, tile[2]], q1x_send.at[t])

        for d in HOPS:
            yd, xd = lax.rem(y + d, 4), lax.rem(x + d, 4)
            for k in range(4):

                @pl.when(has_more(yd, k))
                def _(t=t, d=d, k=k):
                    await_bytes(ea1.at[0, 0, :, tile[2]], s1x_send.at[t, d, k])

            @pl.when(has_more(y, xd))
            def _(t=t, d=d):
                await_bytes(ea1.at[0, :, :, tile[2]], s2x_send.at[t, d])

        for k in range(4):

            @pl.when(has_more(y, k))
            def _(t=t, k=k):
                await_bytes(ea1.at[0, pl.ds(0, 3), :, tile[2]], q2x_send.at[t, k])

        await_bytes(homes[t], o_recv.at[t])


def shards(scale, ensemble, cotangent, w_query, w_key, w_value, w_out):
    shape = ensemble.shape
    full = lambda: pltpu.VMEM((4, 4, ROWS, WIDTH), BF16)
    part = lambda: pltpu.VMEM((4, 4, ROWS, SPAN), BF16)
    square = lambda: pltpu.VMEM((ALL, ALL), BF16)
    small = lambda *lead: pltpu.VMEM((2,) + lead + (MEMBERS // 4, 2 * MEMBERS), F32)
    dma = pltpu.SemaphoreType.DMA
    flat = jax.ShapeDtypeStruct((ROWS, CELL_DEV), BF16)
    hbm = pl.BlockSpec(memory_space=pltpu.HBM)
    branch, grad = pl.pallas_call(
        functools.partial(kernel, scale),
        out_shape=(flat, flat),
        in_specs=[hbm] * 6,
        out_specs=(hbm, hbm),
        scratch_shapes=[pltpu.VMEM((4, CH, CH), BF16)]
        + [part() for _ in range(4)]
        + [full() for _ in range(4)]
        + [part() for _ in range(4)]
        + [pltpu.VMEM((3, ALL, 2 * TILE), F32)]
        + [square() for _ in range(3)]
        + [
            pltpu.VMEM((MEMBERS, ALL), F32),
            pltpu.VMEM((4, CH, 256), F32),
            pltpu.VMEM((ALL, 2 * MEMBERS), BF16),
            pltpu.VMEM((ALL, 2 * MEMBERS), BF16),
            pltpu.VMEM((2, MEMBERS // 2, 2 * MEMBERS), F32),
            small(),
            small(),
            small(3),
            small(),
            small(3),
            small(),
            small(NZ - 1),
            pltpu.VMEM((2, MEMBERS // 2, 2 * MEMBERS), F32),
            pltpu.VMEM((MEMBERS, MEMBERS), F32),
            pltpu.VMEM((MEMBERS, ALL), F32),
            pltpu.VMEM((MEMBERS, ALL), F32),
        ]
        + [
            dma,
            dma((2, 2)),
            dma((2, 2, 3)),
            dma((2, 4, 4)),
            dma((2, 4)),
            dma((2, 2)),
            dma((2, 2, 3)),
            dma((2, 4)),
            dma((2,)),
            dma((2, 2)),
            dma((2, 3, 2)),
            dma((2, 3, 2)),
            dma((2, NZ - 1, 2)),
            dma((2, 2)),
            dma((2, 2)),
            dma((2, 2, 3)),
            dma((2,)),
            dma((2, 4)),
            dma((2, 2)),
            dma((2, 4)),
            dma((2,)),
        ],
        compiler_params=pltpu.CompilerParams(
            collective_id=0, has_side_effects=True, vmem_limit_bytes=67043328
        ),
    )(
        ensemble.reshape(ROWS, CELL_DEV),
        cotangent.reshape(ROWS, CELL_DEV),
        w_query,
        w_key,
        w_value,
        w_out,
    )
    updated = ensemble.astype(F32) + branch.reshape(shape).astype(F32)
    ensemble_grad = cotangent.astype(F32) + grad.reshape(shape).astype(F32)
    return updated, ensemble_grad


def solution(mesh):
    torus = Mesh(mesh.devices.reshape(NY, NX, NZ, NC), ("y", "x", "z", "c"))
    scale = 1.0 / (CELL_DEV * NZ * NC * math.sqrt(CH))
    placed = P(("y", "x"), None, ("z", "c"))
    return jax.shard_map(
        functools.partial(shards, scale),
        mesh=torus,
        in_specs=(placed, placed, P(), P(), P(), P()),
        out_specs=(placed, placed),
        check_vma=False,
    )
```

```python
import functools
import math

import jax
import jax.numpy as jnp
from jax import lax
from jax.experimental import pallas as pl
from jax.experimental.pallas import tpu as pltpu
from jax.sharding import Mesh
from jax.sharding import PartitionSpec as P

MESH = pl.DeviceIdType.MESH
F32 = jnp.float32
BF16 = jnp.bfloat16
HIGH = lax.Precision.HIGHEST

NX, NY, NZ, NC = 4, 4, 8, 2
PEERS = NX * NY
CH = 16
MEM_DEV = 4
ROWS = MEM_DEV * CH
MEMBERS = MEM_DEV * PEERS
ALL = ROWS * PEERS
TILE = 128
MAIN = 5
EXTRA = 10
WIDTH = (MAIN + 1) * TILE
CELL_DEV = 11520
SPAN = 3 * TILE
XLO = MAIN * TILE
HOPS = (1, 3, 2)
PLANE = [(dy, dx) for dy in HOPS + (0,) for dx in HOPS + (0,) if dy or dx]
PLANE.sort(key=lambda d: -(min(d[0], 4 - d[0]) + min(d[1], 4 - d[1])))


def tn(a, b, precision=None):
    return lax.dot_general(
        a, b, (((0,), (0,)), ((), ())), precision=precision, preferred_element_type=F32
    )


def kernel(
    scale,
    e_hbm,
    c_hbm,
    wq_hbm,
    wk_hbm,
    wv_hbm,
    wo_hbm,
    ob,
    og,
    e_out,
    c_out,
    weights_in,
    ea1,
    eb1,
    ca1,
    cb1,
    e_all,
    c_all,
    bm,
    gm,
    ba,
    bb,
    ga,
    gb,
    partial,
    dmat,
    tmat,
    gmat,
    turned,
    acc,
    consts,
    fold_lo,
    fold_hi,
    packed,
    cbuf,
    ysrc,
    ybuf,
    zsrc,
    zbuf,
    fin,
    wsave,
    exp_a,
    exp_b,
    w_sem,
    k_sem,
    s1_send,
    s1_recv,
    s1x_send,
    s1x_recv,
    s2_send,
    s2_recv,
    s2x_send,
    s2x_recv,
    c_sem,
    y_sem,
    z_sem,
    f_sem,
    q1_send,
    q1_recv,
    q1x_send,
    q1x_recv,
    q2_send,
    q2x_send,
    o_recv,
):
    y, x = lax.axis_index("y"), lax.axis_index("x")
    z, c = lax.axis_index("z"), lax.axis_index("c")
    sources = (e_hbm, c_hbm)
    first_a, first_b = (ea1, ca1), (eb1, cb1)
    whole = (e_all, c_all)
    made = (bm, gm)
    back_a, back_b = (ba, ga), (bb, gb)
    homes = (ob, og)

    def at(dy=0, dx=0, dz=0, dc=0):
        return (
            lax.rem(y + dy, NY),
            lax.rem(x + dx, NX),
            lax.rem(z + dz, NZ),
            lax.rem(c + dc, NC),
        )

    def more(yd, xd):
        return 4 * lax.rem(xd + yd + 2 * c, 4) + yd

    def has_more(yd, xd):
        return more(yd, xd) < EXTRA

    def lanes(yd, xd, lo):
        return pl.ds(pl.multiple_of((4 * yd + xd) * XLO + lo, TILE), TILE)

    def more_lanes(yd, xd):
        return pl.ds(pl.multiple_of((MAIN * PEERS + more(yd, xd)) * TILE, TILE), TILE)

    def remote(src, dst, send, recv, device):
        pltpu.make_async_remote_copy(
            src_ref=src, dst_ref=dst, send_sem=send, recv_sem=recv, device_id=device, device_id_type=MESH
        ).start()

    def local(src, dst, sem):
        pltpu.make_async_copy(src, dst, sem).start()

    def await_bytes(view, sem):
        pltpu.make_async_copy(view, view, sem).wait()

    mine = has_more(y, x)
    tile = [pl.ds(TILE * k, TILE) for k in range(6)]

    def out1(t, j):
        src, pa, pb = sources[t], first_a[t], first_b[t]
        for d in HOPS:

            @pl.loop(0, 4)
            def _(k, d=d):
                xd, yd = lax.rem(x + d, 4), lax.rem(y + d, 4)
                remote(
                    src.at[:, lanes(k, xd, TILE * j)],
                    pa.at[k, x, :, tile[j]],
                    s1_send.at[t, 0],
                    s1_recv.at[t, 0, j],
                    at(dx=d),
                )
                if j < 2:
                    remote(
                        src.at[:, lanes(yd, k, SPAN + TILE * j)],
                        pb.at[k, y, :, tile[j]],
                        s1_send.at[t, 1],
                        s1_recv.at[t, 1, j],
                        at(dy=d),
                    )
                else:

                    @pl.when(has_more(yd, k))
                    def _():
                        remote(
                            src.at[:, more_lanes(yd, k)],
                            pb.at[k, y, :, tile[j]],
                            s1x_send.at[t, d, k],
                            s1x_recv.at[t, k],
                            at(dy=d),
                        )

        @pl.loop(0, 4)
        def _(k):
            local(src.at[:, lanes(k, x, TILE * j)], pa.at[k, x, :, tile[j]], s1_recv.at[t, 0, j])
            if j < 2:
                local(src.at[:, lanes(y, k, SPAN + TILE * j)], pb.at[k, y, :, tile[j]], s1_recv.at[t, 1, j])
            else:

                @pl.when(has_more(y, k))
                def _():
                    local(src.at[:, more_lanes(y, k)], pb.at[k, y, :, tile[j]], s1x_recv.at[t, k])

    def out2(t, j):
        pa, pb, dst = first_a[t], first_b[t], whole[t]
        await_bytes(pa.at[:, :, :, tile[j]], s1_recv.at[t, 0, j])
        for d in HOPS:
            yd = lax.rem(y + d, 4)
            remote(
                pa.at[yd, :, :, tile[j]], dst.at[y, :, :, tile[j]], s2_send.at[t, 0], s2_recv.at[t, 0, j], at(dy=d)
            )
        local(pa.at[y, :, :, tile[j]], dst.at[y, :, :, tile[j]], s2_recv.at[t, 0, j])
        if j < 2:
            await_bytes(pb.at[:, :, :, tile[j]], s1_recv.at[t, 1, j])
            for d in HOPS:
                xd = lax.rem(x + d, 4)
                remote(
                    pb.at[xd, :, :, tile[j]],
                    dst.at[:, x, :, tile[3 + j]],
                    s2_send.at[t, 1],
                    s2_recv.at[t, 1, j],
                    at(dx=d),
                )
            local(pb.at[x, :, :, tile[j]], dst.at[:, x, :, tile[3 + j]], s2_recv.at[t, 1, j])
        else:
            for d in HOPS:
                xd = lax.rem(x + d, 4)

                @pl.when(has_more(y, xd))
                def _(d=d, xd=xd):
                    await_bytes(pb.at[xd, :, :, tile[j]], s1x_recv.at[t, xd])
                    remote(
                        pb.at[xd, :, :, tile[j]],
                        dst.at[:, x, :, tile[3 + j]],
                        s2x_send.at[t, d],
                        s2x_recv.at[t],
                        at(dx=d),
                    )

            @pl.when(mine)
            def _():
                await_bytes(pb.at[x, :, :, tile[j]], s1x_recv.at[t, x])
                local(pb.at[x, :, :, tile[j]], dst.at[:, x, :, tile[3 + j]], s2x_recv.at[t])

    def arrived(t, j):
        await_bytes(whole[t].at[:, :, :, tile[j]], s2_recv.at[t, 0, j])
        if j < 2:
            await_bytes(whole[t].at[:, :, :, tile[3 + j]], s2_recv.at[t, 1, j])
        else:

            @pl.when(mine)
            def _():
                await_bytes(whole[t].at[:, :, :, tile[3 + j]], s2x_recv.at[t])

    def home1(t, j):
        src, pa, pb = made[t], back_a[t], back_b[t]
        for d in HOPS:
            yh, xh = lax.rem(y + d, 4), lax.rem(x + d, 4)
            remote(
                src.at[yh, :, :, tile[j]], pa.at[y, :, :, tile[j]], q1_send.at[t, 0], q1_recv.at[t, 0, j], at(dy=d)
            )
            if j < 2:
                remote(
                    src.at[:, xh, :, tile[3 + j]],
                    pb.at[x, :, :, tile[j]],
                    q1_send.at[t, 1],
                    q1_recv.at[t, 1, j],
                    at(dx=d),
                )
        local(src.at[y, :, :, tile[j]], pa.at[y, :, :, tile[j]], q1_recv.at[t, 0, j])
        if j < 2:
            local(src.at[:, x, :, tile[3 + j]], pb.at[x, :, :, tile[j]], q1_recv.at[t, 1, j])
        else:

            @pl.when(mine)
            def _():
                for d in HOPS:
                    xh = lax.rem(x + d, 4)
                    remote(
                        src.at[:, xh, :, tile[3 + j]],
                        pb.at[x, :, :, tile[j]],
                        q1x_send.at[t],
                        q1x_recv.at[t, x],
                        at(dx=d),
                    )
                local(src.at[:, x, :, tile[3 + j]], pb.at[x, :, :, tile[j]], q1x_recv.at[t, x])

    def home2(t, j):
        pa, pb, dst = back_a[t], back_b[t], homes[t]
        await_bytes(pa.at[:, :, :, tile[j]], q1_recv.at[t, 0, j])

        @pl.loop(0, 4)
        def _(s):
            for d in HOPS:
                remote(
                    pa.at[s, lax.rem(x + d, 4), :, tile[j]],
                    dst.at[:, lanes(s, x, TILE * j)],
                    q2_send.at[t, 0],
                    o_recv.at[t],
                    at(dx=d),
                )
            local(pa.at[s, x, :, tile[j]], dst.at[:, lanes(s, x, TILE * j)], o_recv.at[t])

        if j < 2:
            await_bytes(pb.at[:, :, :, tile[j]], q1_recv.at[t, 1, j])

        @pl.loop(0, 4)
        def _(s):
            if j < 2:
                for d in HOPS:
                    remote(
                        pb.at[s, lax.rem(y + d, 4), :, tile[j]],
                        dst.at[:, lanes(y, s, SPAN + TILE * j)],
                        q2_send.at[t, 1],
                        o_recv.at[t],
                        at(dy=d),
                    )
                local(pb.at[s, y, :, tile[j]], dst.at[:, lanes(y, s, SPAN + TILE * j)], o_recv.at[t])
            else:

                @pl.when(has_more(y, s))
                def _():
                    await_bytes(pb.at[s, :, :, tile[j]], q1x_recv.at[t, s])
                    for d in HOPS:
                        remote(
                            pb.at[s, lax.rem(y + d, 4), :, tile[j]],
                            dst.at[:, more_lanes(y, s)],
                            q2x_send.at[t, s],
                            o_recv.at[t],
                            at(dy=d),
                        )
                    local(pb.at[s, y, :, tile[j]], dst.at[:, more_lanes(y, s)], o_recv.at[t])

    def cells(t, j, r=None):
        ref = whole[t]
        if r is None:
            two = [ref[:, :, :, tile[k]].reshape(ALL, TILE) for k in (j, 3 + j)]
        else:
            two = [ref[r, :, :, tile[k]].reshape(256, TILE) for k in (j, 3 + j)]
        return jnp.concatenate(two, axis=1)

    def turn(j):
        for q in range(4):
            turned[j, :, 256 * q : 256 * q + 256] = cells(0, j, q).T

    def gram(t, j, const):
        @pl.loop(0, 4)
        def _(r):
            rows = pl.ds(pl.multiple_of(r * CH, CH), CH)
            left = cells(t, j, r)
            for q in range(4):
                cols = slice(256 * q, 256 * q + 256)
                s = jnp.dot(left, turned[j, :, cols], preferred_element_type=F32)
                s = s.reshape(CH, CH, 256) * consts[const][None]
                s = jnp.sum(s, axis=1)
                if j == 0:
                    acc[t, rows, cols] = s
                else:
                    acc[t, rows, cols] += s

    half = MEMBERS // 4
    own = pl.ds(pl.multiple_of(half * c, half), half)
    other = pl.ds(pl.multiple_of(half * (1 - c), half), half)

    def pack(t):
        rest = acc[t]
        parts = []
        for _ in range(3):
            parts.append(rest.astype(BF16))
            rest = rest - parts[-1].astype(F32)
        h = MEMBERS // 2
        low = jnp.concatenate([p[:h] for p in parts], axis=0)
        high = jnp.concatenate([p[h:] for p in parts], axis=0)
        both = jnp.dot(low, fold_lo[...], preferred_element_type=F32)
        both += jnp.dot(high, fold_hi[...], preferred_element_type=F32)
        packed[t] = both[:h] + both[h : 2 * h] + both[2 * h :]

    def swap(src, dst, send, recv, device):
        return pltpu.make_async_remote_copy(
            src_ref=src, dst_ref=dst, send_sem=send, recv_sem=recv, device_id=device, device_id_type=MESH
        )

    def run(copies):
        for copy in copies:
            copy.start()

    def collect(t, copies, src, buf, dst):
        for copy in copies:
            copy.wait()
        total = src[t]
        for i in range(len(copies)):
            total += buf[t, i]
        if dst is fin:
            fin[t, own] = total
        else:
            dst[t] = total

    def stage(t, name):
        if name == "core":
            return [swap(packed.at[t, other], cbuf.at[t], c_sem.at[t, 0], c_sem.at[t, 1], at(dc=1))]
        if name == "back":
            return [swap(fin.at[t, own], fin.at[t, own], f_sem.at[t, 0], f_sem.at[t, 1], at(dc=1))]
        if name == "plane":
            return [
                swap(ysrc.at[t], ybuf.at[t, i], y_sem.at[t, i, 0], y_sem.at[t, i, 1], at(dy=dy, dx=dx))
                for i, (dy, dx) in enumerate(PLANE)
            ]
        return [
            swap(zsrc.at[t], zbuf.at[t, d - 1], z_sem.at[t, d - 1, 0], z_sem.at[t, d - 1, 1], at(dz=d))
            for d in range(1, NZ)
        ]

    def reduce_begin(t, after_core, after_plane):
        pack(t)
        core = stage(t, "core")
        run(core)
        after_core()
        core[0].wait()
        ysrc[t] = packed[t, own] + cbuf[t]
        plane = stage(t, "plane")
        run(plane)
        after_plane()
        collect(t, plane, ysrc, ybuf, zsrc)
        run(stage(t, "z"))

    def reduce_z(t):
        collect(t, stage(t, "z"), zsrc, zbuf, fin)
        run(stage(t, "back"))

    def reduce_end(t):
        stage(t, "back")[0].wait()
        return jnp.concatenate([fin[t, :, :MEMBERS], fin[t, :, MEMBERS:]], axis=0)

    spread = (
        lax.broadcasted_iota(jnp.int32, (MEMBERS, ALL), 0)
        == lax.broadcasted_iota(jnp.int32, (MEMBERS, ALL), 1) // CH
    ).astype(BF16)

    def blocks(dst, *terms):
        @pl.loop(0, MEMBERS)
        def _(m):
            rows = pl.ds(pl.multiple_of(m * CH, CH), CH)
            for q in range(4):
                cols = slice(256 * q, 256 * q + 256)
                total = None
                for coefficient, const in terms:
                    term = jnp.broadcast_to(coefficient[pl.ds(m, 1), cols], (CH, 256)) * consts[const]
                    total = term if total is None else total + term
                dst[rows, cols] = total.astype(BF16)

    def put(t, j, r, value):
        value = value.astype(BF16)
        made[t][r, :, :, tile[j]] = value[:, :TILE].reshape(4, ROWS, TILE)
        made[t][r, :, :, tile[3 + j]] = value[:, TILE:].reshape(4, ROWS, TILE)

    barrier = pltpu.get_barrier_semaphore()
    partners = [at(dc=1)]
    partners += [at(dy=dy, dx=dx) for dy, dx in PLANE]
    partners += [at(dz=d) for d in range(1, NZ)]
    for device in partners:
        pl.semaphore_signal(barrier, inc=1, device_id=device, device_id_type=MESH)
    for i, ref in enumerate((wq_hbm, wk_hbm, wv_hbm, wo_hbm)):
        local(ref, weights_in.at[i], w_sem)
    pl.semaphore_wait(barrier, len(partners))

    for j in range(3):
        out1(0, j)
    local(e_hbm, e_out, k_sem.at[0])
    local(c_hbm, c_out, k_sem.at[1])

    @pl.when(jnp.logical_not(mine))
    def _():
        e_all[:, :, :, XLO:] = jnp.zeros((4, 4, ROWS, TILE), BF16)
        c_all[:, :, :, XLO:] = jnp.zeros((4, 4, ROWS, TILE), BF16)

    await_bytes(weights_in, w_sem)
    wq, wk, wv, wo = (weights_in[i] for i in range(4))
    a_mat = tn(wq, wk)
    at_mat = tn(wk, wq)
    m_mat = jnp.dot(wo, wv, preferred_element_type=F32)
    mt_mat = lax.dot_general(wv, wo, (((0,), (1,)), ((), ())), preferred_element_type=F32)
    row16 = lax.broadcasted_iota(jnp.int32, (CH, 256), 0)
    lane16 = lax.rem(lax.broadcasted_iota(jnp.int32, (CH, 256), 1), CH)
    repeat = (row16 == lane16).astype(F32)
    for i, mat in enumerate((a_mat, at_mat, m_mat, mt_mat)):
        consts[i] = jnp.dot(mat, repeat, precision=HIGH, preferred_element_type=F32)
    group = lax.broadcasted_iota(jnp.int32, (ALL, 2 * MEMBERS), 0) // CH
    column = lax.broadcasted_iota(jnp.int32, (ALL, 2 * MEMBERS), 1)
    fold_lo[...] = (group == column).astype(BF16)
    fold_hi[...] = (group == column - MEMBERS).astype(BF16)

    for j in range(3):
        out2(0, j)
    out1(1, 0)
    for j in range(3):
        arrived(0, j)
        turn(j)
        gram(0, j, 0)

    def more_cotangent():
        out2(1, 0)
        out1(1, 2)

    reduce_begin(0, lambda: out1(1, 1), more_cotangent)
    out2(1, 1)
    arrived(1, 0)
    gram(1, 0, 2)
    reduce_z(0)
    out2(1, 2)
    scores = scale * reduce_end(0)
    exponent = jnp.exp(scores - jnp.max(scores, axis=1, keepdims=True))
    weights = exponent / jnp.sum(exponent, axis=1, keepdims=True)
    wsave[...] = weights
    w_half = weights.astype(BF16)
    exp_a[...] = jnp.dot(w_half, spread, preferred_element_type=F32)
    blocks(dmat, (exp_a, 2))

    def mix_branch(j):
        right = cells(0, j)
        for r in range(4):
            put(0, j, r, jnp.dot(dmat[256 * r : 256 * r + 256, :], right, preferred_element_type=F32))

    mix_branch(0)
    home1(0, 0)
    for j in (1, 2):
        arrived(1, j)
        gram(1, j, 2)

    def more_branch():
        home1(0, 1)
        mix_branch(2)
        home1(0, 2)
        home2(0, 0)

    reduce_begin(1, lambda: mix_branch(1), more_branch)
    home2(0, 1)
    exp_b[...] = tn(wsave[...].astype(BF16), spread)
    blocks(tmat, (exp_b, 3))
    for j in range(3):
        right = cells(1, j)
        for r in range(4):
            rows = slice(256 * r, 256 * r + 256)
            partial[j, rows, :] = jnp.dot(tmat[rows, :], right, preferred_element_type=F32)
    reduce_z(1)
    home2(0, 2)
    pairs = reduce_end(1)
    weights = wsave[...]
    grad_scores = weights * (pairs - jnp.sum(weights * pairs, axis=1, keepdims=True))
    g_half = (scale * grad_scores).astype(BF16)
    exp_a[...] = jnp.dot(g_half, spread, preferred_element_type=F32)
    exp_b[...] = tn(g_half, spread)
    blocks(gmat, (exp_a, 0), (exp_b, 1))
    for j in range(3):
        right = cells(0, j)
        for r in range(4):
            rows = slice(256 * r, 256 * r + 256)
            out = jnp.dot(gmat[rows, :], right, preferred_element_type=F32)
            put(1, j, r, out + partial[j, rows, :])
        home1(1, j)
    for j in range(3):
        home2(1, j)

    await_bytes(e_out, k_sem.at[0])
    await_bytes(c_out, k_sem.at[1])
    for t in range(2):
        for sem in (s1_send, s2_send, q1_send, q2_send):
            await_bytes(ea1.at[pl.ds(0, 3)], sem.at[t, 0])
            await_bytes(ea1.at[pl.ds(0, 3), :, :, pl.ds(0, 2 * TILE)], sem.at[t, 1])

        @pl.when(mine)
        def _(t=t):
            await_bytes(ea1.at[pl.ds(0, 3), :, :, tile[2]], q1x_send.at[t])

        for d in HOPS:
            yd, xd = lax.rem(y + d, 4), lax.rem(x + d, 4)
            for k in range(4):

                @pl.when(has_more(yd, k))
                def _(t=t, d=d, k=k):
                    await_bytes(ea1.at[0, 0, :, tile[2]], s1x_send.at[t, d, k])

            @pl.when(has_more(y, xd))
            def _(t=t, d=d):
                await_bytes(ea1.at[0, :, :, tile[2]], s2x_send.at[t, d])

        for k in range(4):

            @pl.when(has_more(y, k))
            def _(t=t, k=k):
                await_bytes(ea1.at[0, pl.ds(0, 3), :, tile[2]], q2x_send.at[t, k])

        await_bytes(homes[t], o_recv.at[t])


def shards(scale, ensemble, cotangent, w_query, w_key, w_value, w_out):
    shape = ensemble.shape
    full = lambda: pltpu.VMEM((4, 4, ROWS, WIDTH), BF16)
    part = lambda: pltpu.VMEM((4, 4, ROWS, SPAN), BF16)
    square = lambda: pltpu.VMEM((ALL, ALL), BF16)
    small = lambda *lead: pltpu.VMEM((2,) + lead + (MEMBERS // 4, 2 * MEMBERS), F32)
    dma = pltpu.SemaphoreType.DMA
    flat = pltpu.VMEM((ROWS, CELL_DEV), BF16)
    vmem = pl.BlockSpec(memory_space=pltpu.VMEM)
    hbm = pl.BlockSpec(memory_space=pltpu.HBM)
    branch, grad, ens, cot = pl.pallas_call(
        functools.partial(kernel, scale),
        out_shape=(flat,) * 4,
        in_specs=[hbm] * 6,
        out_specs=(vmem,) * 4,
        scratch_shapes=[pltpu.VMEM((4, CH, CH), BF16)]
        + [part() for _ in range(4)]
        + [full() for _ in range(4)]
        + [part() for _ in range(4)]
        + [pltpu.VMEM((3, ALL, 2 * TILE), F32)]
        + [square() for _ in range(3)]
        + [
            pltpu.VMEM((3, 2 * TILE, ALL), BF16),
            pltpu.VMEM((2, MEMBERS, ALL), F32),
            pltpu.VMEM((4, CH, 256), F32),
            pltpu.VMEM((ALL, 2 * MEMBERS), BF16),
            pltpu.VMEM((ALL, 2 * MEMBERS), BF16),
            pltpu.VMEM((2, MEMBERS // 2, 2 * MEMBERS), F32),
            small(),
            small(),
            small(PEERS - 1),
            small(),
            small(NZ - 1),
            pltpu.VMEM((2, MEMBERS // 2, 2 * MEMBERS), F32),
            pltpu.VMEM((MEMBERS, MEMBERS), F32),
            pltpu.VMEM((MEMBERS, ALL), F32),
            pltpu.VMEM((MEMBERS, ALL), F32),
        ]
        + [
            dma,
            dma((2,)),
            dma((2, 2)),
            dma((2, 2, 3)),
            dma((2, 4, 4)),
            dma((2, 4)),
            dma((2, 2)),
            dma((2, 2, 3)),
            dma((2, 4)),
            dma((2,)),
            dma((2, 2)),
            dma((2, PEERS - 1, 2)),
            dma((2, NZ - 1, 2)),
            dma((2, 2)),
            dma((2, 2)),
            dma((2, 2, 3)),
            dma((2,)),
            dma((2, 4)),
            dma((2, 2)),
            dma((2, 4)),
            dma((2,)),
        ],
        compiler_params=pltpu.CompilerParams(
            collective_id=0, has_side_effects=True, vmem_limit_bytes=67043328 - 4 * ROWS * CELL_DEV * 2
        ),
    )(
        ensemble.reshape(ROWS, CELL_DEV),
        cotangent.reshape(ROWS, CELL_DEV),
        w_query,
        w_key,
        w_value,
        w_out,
    )
    updated = ens.reshape(shape).astype(F32) + branch.reshape(shape).astype(F32)
    ensemble_grad = cot.reshape(shape).astype(F32) + grad.reshape(shape).astype(F32)
    return updated, ensemble_grad


def solution(mesh):
    torus = Mesh(mesh.devices.reshape(NY, NX, NZ, NC), ("y", "x", "z", "c"))
    scale = 1.0 / (CELL_DEV * NZ * NC * math.sqrt(CH))
    placed = P(("y", "x"), None, ("z", "c"))
    return jax.shard_map(
        functools.partial(shards, scale),
        mesh=torus,
        in_specs=(placed, placed, P(), P(), P(), P()),
        out_specs=(placed, placed),
        check_vma=False,
    )
```

```python
import functools
import math

import jax
import jax.numpy as jnp
from jax import lax
from jax.experimental import pallas as pl
from jax.experimental.pallas import tpu as pltpu
from jax.sharding import Mesh
from jax.sharding import PartitionSpec as P

MESH = pl.DeviceIdType.MESH
F32 = jnp.float32
BF16 = jnp.bfloat16
HIGH = lax.Precision.HIGHEST

NX, NY, NZ, NC = 4, 4, 8, 2
PEERS = NX * NY
CH = 16
MEM_DEV = 4
ROWS = MEM_DEV * CH
MEMBERS = MEM_DEV * PEERS
ALL = ROWS * PEERS
TILE = 128
MAIN = 5
EXTRA = 10
WIDTH = (MAIN + 1) * TILE
CELL_DEV = 11520
SPAN = 3 * TILE
XLO = MAIN * TILE
HOPS = (1, 3, 2)
PLANE = [(dy, dx) for dy in HOPS + (0,) for dx in HOPS + (0,) if dy or dx]
PLANE.sort(key=lambda d: -(min(d[0], 4 - d[0]) + min(d[1], 4 - d[1])))


def tn(a, b, precision=None):
    return lax.dot_general(
        a, b, (((0,), (0,)), ((), ())), precision=precision, preferred_element_type=F32
    )


def kernel(
    scale,
    e_hbm,
    c_hbm,
    wq_hbm,
    wk_hbm,
    wv_hbm,
    wo_hbm,
    ob,
    og,
    e_out,
    c_out,
    weights_in,
    ea1,
    eb1,
    ca1,
    cb1,
    e_all,
    c_all,
    bm,
    gm,
    ba,
    bb,
    ga,
    gb,
    partial,
    dmat,
    tmat,
    gmat,
    turned,
    acc,
    consts,
    fold_lo,
    fold_hi,
    packed,
    cbuf,
    ysrc,
    ybuf,
    zsrc,
    zbuf,
    fin,
    wsave,
    exp_a,
    exp_b,
    w_sem,
    k_sem,
    s1_send,
    s1_recv,
    s1x_send,
    s1x_recv,
    s2_send,
    s2_recv,
    s2x_send,
    s2x_recv,
    c_sem,
    y_sem,
    z_sem,
    f_sem,
    q1_send,
    q1_recv,
    q1x_send,
    q1x_recv,
    q2_send,
    q2x_send,
    o_recv,
):
    y, x = lax.axis_index("y"), lax.axis_index("x")
    z, c = lax.axis_index("z"), lax.axis_index("c")
    sources = (e_hbm, c_hbm)
    first_a, first_b = (ea1, ca1), (eb1, cb1)
    whole = (e_all, c_all)
    made = (bm, gm)
    back_a, back_b = (ba, ga), (bb, gb)
    homes = (ob, og)

    def at(dy=0, dx=0, dz=0, dc=0):
        return (
            lax.rem(y + dy, NY),
            lax.rem(x + dx, NX),
            lax.rem(z + dz, NZ),
            lax.rem(c + dc, NC),
        )

    def more(yd, xd):
        return 4 * lax.rem(xd + yd, 4) + lax.rem(yd + 2 * c, 4)

    def has_more(yd, xd):
        return more(yd, xd) < EXTRA

    def lanes(yd, xd, lo):
        return pl.ds(pl.multiple_of((4 * yd + xd) * XLO + lo, TILE), TILE)

    def more_lanes(yd, xd):
        return pl.ds(pl.multiple_of((MAIN * PEERS + more(yd, xd)) * TILE, TILE), TILE)

    def remote(src, dst, send, recv, device):
        pltpu.make_async_remote_copy(
            src_ref=src, dst_ref=dst, send_sem=send, recv_sem=recv, device_id=device, device_id_type=MESH
        ).start()

    def local(src, dst, sem):
        pltpu.make_async_copy(src, dst, sem).start()

    def await_bytes(view, sem):
        pltpu.make_async_copy(view, view, sem).wait()

    mine = has_more(y, x)
    tile = [pl.ds(TILE * k, TILE) for k in range(6)]

    def out1(t, j):
        src, pa, pb = sources[t], first_a[t], first_b[t]
        for d in HOPS:

            @pl.loop(0, 4)
            def _(k, d=d):
                xd, yd = lax.rem(x + d, 4), lax.rem(y + d, 4)
                remote(
                    src.at[:, lanes(k, xd, TILE * j)],
                    pa.at[k, x, :, tile[j]],
                    s1_send.at[t, 0],
                    s1_recv.at[t, 0, j],
                    at(dx=d),
                )
                if j < 2:
                    remote(
                        src.at[:, lanes(yd, k, SPAN + TILE * j)],
                        pb.at[k, y, :, tile[j]],
                        s1_send.at[t, 1],
                        s1_recv.at[t, 1, j],
                        at(dy=d),
                    )
                else:

                    @pl.when(has_more(yd, k))
                    def _():
                        remote(
                            src.at[:, more_lanes(yd, k)],
                            pb.at[k, y, :, tile[j]],
                            s1x_send.at[t, d, k],
                            s1x_recv.at[t, k],
                            at(dy=d),
                        )

        @pl.loop(0, 4)
        def _(k):
            local(src.at[:, lanes(k, x, TILE * j)], pa.at[k, x, :, tile[j]], s1_recv.at[t, 0, j])
            if j < 2:
                local(src.at[:, lanes(y, k, SPAN + TILE * j)], pb.at[k, y, :, tile[j]], s1_recv.at[t, 1, j])
            else:

                @pl.when(has_more(y, k))
                def _():
                    local(src.at[:, more_lanes(y, k)], pb.at[k, y, :, tile[j]], s1x_recv.at[t, k])

    def out2(t, j):
        pa, pb, dst = first_a[t], first_b[t], whole[t]
        await_bytes(pa.at[:, :, :, tile[j]], s1_recv.at[t, 0, j])
        for d in HOPS:
            yd = lax.rem(y + d, 4)
            remote(
                pa.at[yd, :, :, tile[j]], dst.at[y, :, :, tile[j]], s2_send.at[t, 0], s2_recv.at[t, 0, j], at(dy=d)
            )
        local(pa.at[y, :, :, tile[j]], dst.at[y, :, :, tile[j]], s2_recv.at[t, 0, j])
        if j < 2:
            await_bytes(pb.at[:, :, :, tile[j]], s1_recv.at[t, 1, j])
            for d in HOPS:
                xd = lax.rem(x + d, 4)
                remote(
                    pb.at[xd, :, :, tile[j]],
                    dst.at[:, x, :, tile[3 + j]],
                    s2_send.at[t, 1],
                    s2_recv.at[t, 1, j],
                    at(dx=d),
                )
            local(pb.at[x, :, :, tile[j]], dst.at[:, x, :, tile[3 + j]], s2_recv.at[t, 1, j])
        else:
            for d in HOPS:
                xd = lax.rem(x + d, 4)

                @pl.when(has_more(y, xd))
                def _(d=d, xd=xd):
                    await_bytes(pb.at[xd, :, :, tile[j]], s1x_recv.at[t, xd])
                    remote(
                        pb.at[xd, :, :, tile[j]],
                        dst.at[:, x, :, tile[3 + j]],
                        s2x_send.at[t, d],
                        s2x_recv.at[t],
                        at(dx=d),
                    )

            @pl.when(mine)
            def _():
                await_bytes(pb.at[x, :, :, tile[j]], s1x_recv.at[t, x])
                local(pb.at[x, :, :, tile[j]], dst.at[:, x, :, tile[3 + j]], s2x_recv.at[t])

    def arrived(t, j):
        await_bytes(whole[t].at[:, :, :, tile[j]], s2_recv.at[t, 0, j])
        if j < 2:
            await_bytes(whole[t].at[:, :, :, tile[3 + j]], s2_recv.at[t, 1, j])
        else:

            @pl.when(mine)
            def _():
                await_bytes(whole[t].at[:, :, :, tile[3 + j]], s2x_recv.at[t])

    def home1(t, j):
        src, pa, pb = made[t], back_a[t], back_b[t]
        for d in HOPS:
            yh, xh = lax.rem(y + d, 4), lax.rem(x + d, 4)
            remote(
                src.at[yh, :, :, tile[j]], pa.at[y, :, :, tile[j]], q1_send.at[t, 0], q1_recv.at[t, 0, j], at(dy=d)
            )
            if j < 2:
                remote(
                    src.at[:, xh, :, tile[3 + j]],
                    pb.at[x, :, :, tile[j]],
                    q1_send.at[t, 1],
                    q1_recv.at[t, 1, j],
                    at(dx=d),
                )
        local(src.at[y, :, :, tile[j]], pa.at[y, :, :, tile[j]], q1_recv.at[t, 0, j])
        if j < 2:
            local(src.at[:, x, :, tile[3 + j]], pb.at[x, :, :, tile[j]], q1_recv.at[t, 1, j])
        else:

            @pl.when(mine)
            def _():
                for d in HOPS:
                    xh = lax.rem(x + d, 4)
                    remote(
                        src.at[:, xh, :, tile[3 + j]],
                        pb.at[x, :, :, tile[j]],
                        q1x_send.at[t],
                        q1x_recv.at[t, x],
                        at(dx=d),
                    )
                local(src.at[:, x, :, tile[3 + j]], pb.at[x, :, :, tile[j]], q1x_recv.at[t, x])

    def home2(t, j):
        pa, pb, dst = back_a[t], back_b[t], homes[t]
        await_bytes(pa.at[:, :, :, tile[j]], q1_recv.at[t, 0, j])

        @pl.loop(0, 4)
        def _(s):
            for d in HOPS:
                remote(
                    pa.at[s, lax.rem(x + d, 4), :, tile[j]],
                    dst.at[:, lanes(s, x, TILE * j)],
                    q2_send.at[t, 0],
                    o_recv.at[t],
                    at(dx=d),
                )
            local(pa.at[s, x, :, tile[j]], dst.at[:, lanes(s, x, TILE * j)], o_recv.at[t])

        if j < 2:
            await_bytes(pb.at[:, :, :, tile[j]], q1_recv.at[t, 1, j])

        @pl.loop(0, 4)
        def _(s):
            if j < 2:
                for d in HOPS:
                    remote(
                        pb.at[s, lax.rem(y + d, 4), :, tile[j]],
                        dst.at[:, lanes(y, s, SPAN + TILE * j)],
                        q2_send.at[t, 1],
                        o_recv.at[t],
                        at(dy=d),
                    )
                local(pb.at[s, y, :, tile[j]], dst.at[:, lanes(y, s, SPAN + TILE * j)], o_recv.at[t])
            else:

                @pl.when(has_more(y, s))
                def _():
                    await_bytes(pb.at[s, :, :, tile[j]], q1x_recv.at[t, s])
                    for d in HOPS:
                        remote(
                            pb.at[s, lax.rem(y + d, 4), :, tile[j]],
                            dst.at[:, more_lanes(y, s)],
                            q2x_send.at[t, s],
                            o_recv.at[t],
                            at(dy=d),
                        )
                    local(pb.at[s, y, :, tile[j]], dst.at[:, more_lanes(y, s)], o_recv.at[t])

    def cells(t, j, r=None):
        ref = whole[t]
        if r is None:
            two = [ref[:, :, :, tile[k]].reshape(ALL, TILE) for k in (j, 3 + j)]
        else:
            two = [ref[r, :, :, tile[k]].reshape(256, TILE) for k in (j, 3 + j)]
        return jnp.concatenate(two, axis=1)

    def turn(j):
        for q in range(4):
            turned[j, :, 256 * q : 256 * q + 256] = cells(0, j, q).T

    def gram(t, j, const):
        @pl.loop(0, 4)
        def _(r):
            rows = pl.ds(pl.multiple_of(r * CH, CH), CH)
            left = cells(t, j, r)
            for q in range(4):
                cols = slice(256 * q, 256 * q + 256)
                s = jnp.dot(left, turned[j, :, cols], preferred_element_type=F32)
                s = s.reshape(CH, CH, 256) * consts[const][None]
                s = jnp.sum(s, axis=1)
                if j == 0:
                    acc[t, rows, cols] = s
                else:
                    acc[t, rows, cols] += s

    half = MEMBERS // 4
    own = pl.ds(pl.multiple_of(half * c, half), half)
    other = pl.ds(pl.multiple_of(half * (1 - c), half), half)

    def pack(t):
        rest = acc[t]
        parts = []
        for _ in range(3):
            parts.append(rest.astype(BF16))
            rest = rest - parts[-1].astype(F32)
        h = MEMBERS // 2
        low = jnp.concatenate([p[:h] for p in parts], axis=0)
        high = jnp.concatenate([p[h:] for p in parts], axis=0)
        both = jnp.dot(low, fold_lo[...], preferred_element_type=F32)
        both += jnp.dot(high, fold_hi[...], preferred_element_type=F32)
        packed[t] = both[:h] + both[h : 2 * h] + both[2 * h :]

    def swap(src, dst, send, recv, device):
        return pltpu.make_async_remote_copy(
            src_ref=src, dst_ref=dst, send_sem=send, recv_sem=recv, device_id=device, device_id_type=MESH
        )

    def run(copies):
        for copy in copies:
            copy.start()

    def collect(t, copies, src, buf, dst):
        for copy in copies:
            copy.wait()
        total = src[t]
        for i in range(len(copies)):
            total += buf[t, i]
        if dst is fin:
            fin[t, own] = total
        else:
            dst[t] = total

    def stage(t, name):
        if name == "core":
            return [swap(packed.at[t, other], cbuf.at[t], c_sem.at[t, 0], c_sem.at[t, 1], at(dc=1))]
        if name == "back":
            return [swap(fin.at[t, own], fin.at[t, own], f_sem.at[t, 0], f_sem.at[t, 1], at(dc=1))]
        if name == "plane":
            return [
                swap(ysrc.at[t], ybuf.at[t, i], y_sem.at[t, i, 0], y_sem.at[t, i, 1], at(dy=dy, dx=dx))
                for i, (dy, dx) in enumerate(PLANE)
            ]
        return [
            swap(zsrc.at[t], zbuf.at[t, d - 1], z_sem.at[t, d - 1, 0], z_sem.at[t, d - 1, 1], at(dz=d))
            for d in range(1, NZ)
        ]

    def reduce_begin(t, after_core, after_plane):
        pack(t)
        core = stage(t, "core")
        run(core)
        after_core()
        core[0].wait()
        ysrc[t] = packed[t, own] + cbuf[t]
        plane = stage(t, "plane")
        run(plane)
        after_plane()
        collect(t, plane, ysrc, ybuf, zsrc)
        run(stage(t, "z"))

    def reduce_z(t):
        collect(t, stage(t, "z"), zsrc, zbuf, fin)
        run(stage(t, "back"))

    def reduce_end(t):
        stage(t, "back")[0].wait()
        return jnp.concatenate([fin[t, :, :MEMBERS], fin[t, :, MEMBERS:]], axis=0)

    spread = (
        lax.broadcasted_iota(jnp.int32, (MEMBERS, ALL), 0)
        == lax.broadcasted_iota(jnp.int32, (MEMBERS, ALL), 1) // CH
    ).astype(BF16)

    def blocks(dst, *terms):
        @pl.loop(0, MEMBERS)
        def _(m):
            rows = pl.ds(pl.multiple_of(m * CH, CH), CH)
            for q in range(4):
                cols = slice(256 * q, 256 * q + 256)
                total = None
                for coefficient, const in terms:
                    term = jnp.broadcast_to(coefficient[pl.ds(m, 1), cols], (CH, 256)) * consts[const]
                    total = term if total is None else total + term
                dst[rows, cols] = total.astype(BF16)

    def put(t, j, r, value):
        value = value.astype(BF16)
        made[t][r, :, :, tile[j]] = value[:, :TILE].reshape(4, ROWS, TILE)
        made[t][r, :, :, tile[3 + j]] = value[:, TILE:].reshape(4, ROWS, TILE)

    barrier = pltpu.get_barrier_semaphore()
    partners = [at(dc=1)]
    partners += [at(dy=dy, dx=dx) for dy, dx in PLANE]
    partners += [at(dz=d) for d in range(1, NZ)]
    for device in partners:
        pl.semaphore_signal(barrier, inc=1, device_id=device, device_id_type=MESH)
    for i, ref in enumerate((wq_hbm, wk_hbm, wv_hbm, wo_hbm)):
        local(ref, weights_in.at[i], w_sem)
    pl.semaphore_wait(barrier, len(partners))

    for j in range(3):
        out1(0, j)
    local(e_hbm, e_out, k_sem.at[0])
    local(c_hbm, c_out, k_sem.at[1])

    @pl.when(jnp.logical_not(mine))
    def _():
        e_all[:, :, :, XLO:] = jnp.zeros((4, 4, ROWS, TILE), BF16)
        c_all[:, :, :, XLO:] = jnp.zeros((4, 4, ROWS, TILE), BF16)

    await_bytes(weights_in, w_sem)
    wq, wk, wv, wo = (weights_in[i] for i in range(4))
    a_mat = tn(wq, wk)
    at_mat = tn(wk, wq)
    m_mat = jnp.dot(wo, wv, preferred_element_type=F32)
    mt_mat = lax.dot_general(wv, wo, (((0,), (1,)), ((), ())), preferred_element_type=F32)
    row16 = lax.broadcasted_iota(jnp.int32, (CH, 256), 0)
    lane16 = lax.rem(lax.broadcasted_iota(jnp.int32, (CH, 256), 1), CH)
    repeat = (row16 == lane16).astype(F32)
    for i, mat in enumerate((a_mat, at_mat, m_mat, mt_mat)):
        consts[i] = jnp.dot(mat, repeat, precision=HIGH, preferred_element_type=F32)
    group = lax.broadcasted_iota(jnp.int32, (ALL, 2 * MEMBERS), 0) // CH
    column = lax.broadcasted_iota(jnp.int32, (ALL, 2 * MEMBERS), 1)
    fold_lo[...] = (group == column).astype(BF16)
    fold_hi[...] = (group == column - MEMBERS).astype(BF16)

    for j in range(3):
        out2(0, j)
    for j in range(3):
        arrived(0, j)
        if j < 2:
            out1(1, j)
        turn(j)
        gram(0, j, 0)

    def more_cotangent():
        out1(1, 2)
        out2(1, 0)

    reduce_begin(0, lambda: None, more_cotangent)
    out2(1, 1)
    out2(1, 2)
    reduce_z(0)
    arrived(1, 0)
    gram(1, 0, 2)
    scores = scale * reduce_end(0)
    exponent = jnp.exp(scores - jnp.max(scores, axis=1, keepdims=True))
    weights = exponent / jnp.sum(exponent, axis=1, keepdims=True)
    wsave[...] = weights
    w_half = weights.astype(BF16)
    exp_a[...] = jnp.dot(w_half, spread, preferred_element_type=F32)
    blocks(dmat, (exp_a, 2))

    def mix_branch(j):
        right = cells(0, j)
        for r in range(4):
            put(0, j, r, jnp.dot(dmat[256 * r : 256 * r + 256, :], right, preferred_element_type=F32))

    mix_branch(0)
    home1(0, 0)
    arrived(1, 1)
    gram(1, 1, 2)
    mix_branch(1)
    home1(0, 1)
    arrived(1, 2)
    gram(1, 2, 2)

    def more_branch():
        home2(0, 0)
        home1(0, 2)

    reduce_begin(1, lambda: mix_branch(2), more_branch)
    exp_b[...] = tn(wsave[...].astype(BF16), spread)
    blocks(tmat, (exp_b, 3))
    for j in range(3):
        right = cells(1, j)
        for r in range(4):
            rows = slice(256 * r, 256 * r + 256)
            partial[j, rows, :] = jnp.dot(tmat[rows, :], right, preferred_element_type=F32)
    home2(0, 1)
    reduce_z(1)
    home2(0, 2)
    pairs = reduce_end(1)
    weights = wsave[...]
    grad_scores = weights * (pairs - jnp.sum(weights * pairs, axis=1, keepdims=True))
    g_half = (scale * grad_scores).astype(BF16)
    exp_a[...] = jnp.dot(g_half, spread, preferred_element_type=F32)
    exp_b[...] = tn(g_half, spread)
    blocks(gmat, (exp_a, 0), (exp_b, 1))
    for j in range(3):
        right = cells(0, j)
        for r in range(4):
            rows = slice(256 * r, 256 * r + 256)
            out = jnp.dot(gmat[rows, :], right, preferred_element_type=F32)
            put(1, j, r, out + partial[j, rows, :])
        home1(1, j)
    for j in range(3):
        home2(1, j)

    await_bytes(e_out, k_sem.at[0])
    await_bytes(c_out, k_sem.at[1])
    for t in range(2):
        for sem in (s1_send, s2_send, q1_send, q2_send):
            await_bytes(ea1.at[pl.ds(0, 3)], sem.at[t, 0])
            await_bytes(ea1.at[pl.ds(0, 3), :, :, pl.ds(0, 2 * TILE)], sem.at[t, 1])

        @pl.when(mine)
        def _(t=t):
            await_bytes(ea1.at[pl.ds(0, 3), :, :, tile[2]], q1x_send.at[t])

        for d in HOPS:
            yd, xd = lax.rem(y + d, 4), lax.rem(x + d, 4)
            for k in range(4):

                @pl.when(has_more(yd, k))
                def _(t=t, d=d, k=k):
                    await_bytes(ea1.at[0, 0, :, tile[2]], s1x_send.at[t, d, k])

            @pl.when(has_more(y, xd))
            def _(t=t, d=d):
                await_bytes(ea1.at[0, :, :, tile[2]], s2x_send.at[t, d])

        for k in range(4):

            @pl.when(has_more(y, k))
            def _(t=t, k=k):
                await_bytes(ea1.at[0, pl.ds(0, 3), :, tile[2]], q2x_send.at[t, k])

        await_bytes(homes[t], o_recv.at[t])


def shards(scale, ensemble, cotangent, w_query, w_key, w_value, w_out):
    shape = ensemble.shape
    full = lambda: pltpu.VMEM((4, 4, ROWS, WIDTH), BF16)
    part = lambda: pltpu.VMEM((4, 4, ROWS, SPAN), BF16)
    square = lambda: pltpu.VMEM((ALL, ALL), BF16)
    small = lambda *lead: pltpu.VMEM((2,) + lead + (MEMBERS // 4, 2 * MEMBERS), F32)
    dma = pltpu.SemaphoreType.DMA
    flat = pltpu.VMEM((ROWS, CELL_DEV), BF16)
    vmem = pl.BlockSpec(memory_space=pltpu.VMEM)
    hbm = pl.BlockSpec(memory_space=pltpu.HBM)
    branch, grad, ens, cot = pl.pallas_call(
        functools.partial(kernel, scale),
        out_shape=(flat,) * 4,
        in_specs=[hbm] * 6,
        out_specs=(vmem,) * 4,
        scratch_shapes=[pltpu.VMEM((4, CH, CH), BF16)]
        + [part() for _ in range(4)]
        + [full() for _ in range(4)]
        + [part() for _ in range(4)]
        + [pltpu.VMEM((3, ALL, 2 * TILE), F32)]
        + [square() for _ in range(3)]
        + [
            pltpu.VMEM((3, 2 * TILE, ALL), BF16),
            pltpu.VMEM((2, MEMBERS, ALL), F32),
            pltpu.VMEM((4, CH, 256), F32),
            pltpu.VMEM((ALL, 2 * MEMBERS), BF16),
            pltpu.VMEM((ALL, 2 * MEMBERS), BF16),
            pltpu.VMEM((2, MEMBERS // 2, 2 * MEMBERS), F32),
            small(),
            small(),
            small(PEERS - 1),
            small(),
            small(NZ - 1),
            pltpu.VMEM((2, MEMBERS // 2, 2 * MEMBERS), F32),
            pltpu.VMEM((MEMBERS, MEMBERS), F32),
            pltpu.VMEM((MEMBERS, ALL), F32),
            pltpu.VMEM((MEMBERS, ALL), F32),
        ]
        + [
            dma,
            dma((2,)),
            dma((2, 2)),
            dma((2, 2, 3)),
            dma((2, 4, 4)),
            dma((2, 4)),
            dma((2, 2)),
            dma((2, 2, 3)),
            dma((2, 4)),
            dma((2,)),
            dma((2, 2)),
            dma((2, PEERS - 1, 2)),
            dma((2, NZ - 1, 2)),
            dma((2, 2)),
            dma((2, 2)),
            dma((2, 2, 3)),
            dma((2,)),
            dma((2, 4)),
            dma((2, 2)),
            dma((2, 4)),
            dma((2,)),
        ],
        compiler_params=pltpu.CompilerParams(
            collective_id=0, has_side_effects=True, vmem_limit_bytes=67043328 - 4 * ROWS * CELL_DEV * 2
        ),
    )(
        ensemble.reshape(ROWS, CELL_DEV),
        cotangent.reshape(ROWS, CELL_DEV),
        w_query,
        w_key,
        w_value,
        w_out,
    )
    updated = ens.reshape(shape).astype(F32) + branch.reshape(shape).astype(F32)
    ensemble_grad = cot.reshape(shape).astype(F32) + grad.reshape(shape).astype(F32)
    return updated, ensemble_grad


def solution(mesh):
    torus = Mesh(mesh.devices.reshape(NY, NX, NZ, NC), ("y", "x", "z", "c"))
    scale = 1.0 / (CELL_DEV * NZ * NC * math.sqrt(CH))
    placed = P(("y", "x"), None, ("z", "c"))
    return jax.shard_map(
        functools.partial(shards, scale),
        mesh=torus,
        in_specs=(placed, placed, P(), P(), P(), P()),
        out_specs=(placed, placed),
        check_vma=False,
    )
```

```python
import functools
import math

import jax
import jax.numpy as jnp
from jax import lax
from jax.experimental import pallas as pl
from jax.experimental.pallas import tpu as pltpu
from jax.sharding import Mesh
from jax.sharding import PartitionSpec as P

MESH = pl.DeviceIdType.MESH
F32 = jnp.float32
BF16 = jnp.bfloat16
HIGH = lax.Precision.HIGHEST

NX, NY, NZ, NC = 4, 4, 8, 2
PEERS = NX * NY
CH = 16
MEM_DEV = 4
ROWS = MEM_DEV * CH
MEMBERS = MEM_DEV * PEERS
ALL = ROWS * PEERS
TILE = 128
MAIN = 5
EXTRA = 10
WIDTH = (MAIN + 1) * TILE
CELL_DEV = 11520
SPAN = 3 * TILE
XLO = MAIN * TILE
HOPS = (1, 3, 2)
PLANE = [(dy, dx) for dy in HOPS + (0,) for dx in HOPS + (0,) if dy or dx]
PLANE.sort(key=lambda d: -(min(d[0], 4 - d[0]) + min(d[1], 4 - d[1])))


def tn(a, b, precision=None):
    return lax.dot_general(
        a, b, (((0,), (0,)), ((), ())), precision=precision, preferred_element_type=F32
    )


def kernel(
    scale,
    e_hbm,
    c_hbm,
    wq_hbm,
    wk_hbm,
    wv_hbm,
    wo_hbm,
    ob,
    og,
    e_out,
    c_out,
    weights_in,
    ea1,
    eb1,
    ca1,
    cb1,
    e_all,
    c_all,
    bm,
    gm,
    ba,
    bb,
    ga,
    gb,
    partial,
    dmat,
    tmat,
    gmat,
    turned,
    acc,
    consts,
    fold_lo,
    fold_hi,
    packed,
    cbuf,
    ysrc,
    ybuf,
    zsrc,
    zbuf,
    fin,
    wsave,
    exp_a,
    exp_b,
    w_sem,
    k_sem,
    s1_send,
    s1_recv,
    s1x_send,
    s1x_recv,
    s2_send,
    s2_recv,
    s2x_send,
    s2x_recv,
    c_sem,
    y_sem,
    z_sem,
    f_sem,
    q1_send,
    q1_recv,
    q1x_send,
    q1x_recv,
    q2_send,
    q2x_send,
    o_recv,
):
    y, x = lax.axis_index("y"), lax.axis_index("x")
    z, c = lax.axis_index("z"), lax.axis_index("c")
    sources = (e_hbm, c_hbm)
    first_a, first_b = (ea1, ca1), (eb1, cb1)
    whole = (e_all, c_all)
    made = (bm, gm)
    back_a, back_b = (ba, ga), (bb, gb)
    homes = (ob, og)

    def at(dy=0, dx=0, dz=0, dc=0):
        return (
            lax.rem(y + dy, NY),
            lax.rem(x + dx, NX),
            lax.rem(z + dz, NZ),
            lax.rem(c + dc, NC),
        )

    def more(yd, xd):
        return 4 * lax.rem(xd + yd, 4) + lax.rem(yd + 2 * c, 4)

    def has_more(yd, xd):
        return more(yd, xd) < EXTRA

    def lanes(yd, xd, lo):
        return pl.ds(pl.multiple_of((4 * yd + xd) * XLO + lo, TILE), TILE)

    def more_lanes(yd, xd):
        return pl.ds(pl.multiple_of((MAIN * PEERS + more(yd, xd)) * TILE, TILE), TILE)

    def remote(src, dst, send, recv, device):
        pltpu.make_async_remote_copy(
            src_ref=src, dst_ref=dst, send_sem=send, recv_sem=recv, device_id=device, device_id_type=MESH
        ).start()

    def local(src, dst, sem):
        pltpu.make_async_copy(src, dst, sem).start()

    def await_bytes(view, sem):
        pltpu.make_async_copy(view, view, sem).wait()

    mine = has_more(y, x)
    tile = [pl.ds(TILE * k, TILE) for k in range(6)]

    def out1(t, j):
        src, pa, pb = sources[t], first_a[t], first_b[t]
        for d in HOPS:

            @pl.loop(0, 4)
            def _(k, d=d):
                xd, yd = lax.rem(x + d, 4), lax.rem(y + d, 4)
                remote(
                    src.at[:, lanes(k, xd, TILE * j)],
                    pa.at[k, x, :, tile[j]],
                    s1_send.at[t, 0],
                    s1_recv.at[t, 0, j],
                    at(dx=d),
                )
                if j < 2:
                    remote(
                        src.at[:, lanes(yd, k, SPAN + TILE * j)],
                        pb.at[k, y, :, tile[j]],
                        s1_send.at[t, 1],
                        s1_recv.at[t, 1, j],
                        at(dy=d),
                    )
                else:

                    @pl.when(has_more(yd, k))
                    def _():
                        remote(
                            src.at[:, more_lanes(yd, k)],
                            pb.at[k, y, :, tile[j]],
                            s1x_send.at[t, d, k],
                            s1x_recv.at[t, k],
                            at(dy=d),
                        )

        @pl.loop(0, 4)
        def _(k):
            local(src.at[:, lanes(k, x, TILE * j)], pa.at[k, x, :, tile[j]], s1_recv.at[t, 0, j])
            if j < 2:
                local(src.at[:, lanes(y, k, SPAN + TILE * j)], pb.at[k, y, :, tile[j]], s1_recv.at[t, 1, j])
            else:

                @pl.when(has_more(y, k))
                def _():
                    local(src.at[:, more_lanes(y, k)], pb.at[k, y, :, tile[j]], s1x_recv.at[t, k])

    def out2(t, j):
        pa, pb, dst = first_a[t], first_b[t], whole[t]
        await_bytes(pa.at[:, :, :, tile[j]], s1_recv.at[t, 0, j])
        for d in HOPS:
            yd = lax.rem(y + d, 4)
            remote(
                pa.at[yd, :, :, tile[j]], dst.at[y, :, :, tile[j]], s2_send.at[t, 0], s2_recv.at[t, 0, j], at(dy=d)
            )
        local(pa.at[y, :, :, tile[j]], dst.at[y, :, :, tile[j]], s2_recv.at[t, 0, j])
        if j < 2:
            await_bytes(pb.at[:, :, :, tile[j]], s1_recv.at[t, 1, j])
            for d in HOPS:
                xd = lax.rem(x + d, 4)
                remote(
                    pb.at[xd, :, :, tile[j]],
                    dst.at[:, x, :, tile[3 + j]],
                    s2_send.at[t, 1],
                    s2_recv.at[t, 1, j],
                    at(dx=d),
                )
            local(pb.at[x, :, :, tile[j]], dst.at[:, x, :, tile[3 + j]], s2_recv.at[t, 1, j])
        else:
            for d in HOPS:
                xd = lax.rem(x + d, 4)

                @pl.when(has_more(y, xd))
                def _(d=d, xd=xd):
                    await_bytes(pb.at[xd, :, :, tile[j]], s1x_recv.at[t, xd])
                    remote(
                        pb.at[xd, :, :, tile[j]],
                        dst.at[:, x, :, tile[3 + j]],
                        s2x_send.at[t, d],
                        s2x_recv.at[t],
                        at(dx=d),
                    )

            @pl.when(mine)
            def _():
                await_bytes(pb.at[x, :, :, tile[j]], s1x_recv.at[t, x])
                local(pb.at[x, :, :, tile[j]], dst.at[:, x, :, tile[3 + j]], s2x_recv.at[t])

    def arrived(t, j):
        await_bytes(whole[t].at[:, :, :, tile[j]], s2_recv.at[t, 0, j])
        if j < 2:
            await_bytes(whole[t].at[:, :, :, tile[3 + j]], s2_recv.at[t, 1, j])
        else:

            @pl.when(mine)
            def _():
                await_bytes(whole[t].at[:, :, :, tile[3 + j]], s2x_recv.at[t])

    def home1(t, j):
        src, pa, pb = made[t], back_a[t], back_b[t]
        for d in HOPS:
            yh, xh = lax.rem(y + d, 4), lax.rem(x + d, 4)
            remote(
                src.at[yh, :, :, tile[j]], pa.at[y, :, :, tile[j]], q1_send.at[t, 0], q1_recv.at[t, 0, j], at(dy=d)
            )
            if j < 2:
                remote(
                    src.at[:, xh, :, tile[3 + j]],
                    pb.at[x, :, :, tile[j]],
                    q1_send.at[t, 1],
                    q1_recv.at[t, 1, j],
                    at(dx=d),
                )
        local(src.at[y, :, :, tile[j]], pa.at[y, :, :, tile[j]], q1_recv.at[t, 0, j])
        if j < 2:
            local(src.at[:, x, :, tile[3 + j]], pb.at[x, :, :, tile[j]], q1_recv.at[t, 1, j])
        else:

            @pl.when(mine)
            def _():
                for d in HOPS:
                    xh = lax.rem(x + d, 4)
                    remote(
                        src.at[:, xh, :, tile[3 + j]],
                        pb.at[x, :, :, tile[j]],
                        q1x_send.at[t],
                        q1x_recv.at[t, x],
                        at(dx=d),
                    )
                local(src.at[:, x, :, tile[3 + j]], pb.at[x, :, :, tile[j]], q1x_recv.at[t, x])

    def home2(t, j):
        pa, pb, dst = back_a[t], back_b[t], homes[t]
        await_bytes(pa.at[:, :, :, tile[j]], q1_recv.at[t, 0, j])

        @pl.loop(0, 4)
        def _(s):
            for d in HOPS:
                remote(
                    pa.at[s, lax.rem(x + d, 4), :, tile[j]],
                    dst.at[:, lanes(s, x, TILE * j)],
                    q2_send.at[t, 0],
                    o_recv.at[t],
                    at(dx=d),
                )
            local(pa.at[s, x, :, tile[j]], dst.at[:, lanes(s, x, TILE * j)], o_recv.at[t])

        if j < 2:
            await_bytes(pb.at[:, :, :, tile[j]], q1_recv.at[t, 1, j])

        @pl.loop(0, 4)
        def _(s):
            if j < 2:
                for d in HOPS:
                    remote(
                        pb.at[s, lax.rem(y + d, 4), :, tile[j]],
                        dst.at[:, lanes(y, s, SPAN + TILE * j)],
                        q2_send.at[t, 1],
                        o_recv.at[t],
                        at(dy=d),
                    )
                local(pb.at[s, y, :, tile[j]], dst.at[:, lanes(y, s, SPAN + TILE * j)], o_recv.at[t])
            else:

                @pl.when(has_more(y, s))
                def _():
                    await_bytes(pb.at[s, :, :, tile[j]], q1x_recv.at[t, s])
                    for d in HOPS:
                        remote(
                            pb.at[s, lax.rem(y + d, 4), :, tile[j]],
                            dst.at[:, more_lanes(y, s)],
                            q2x_send.at[t, s],
                            o_recv.at[t],
                            at(dy=d),
                        )
                    local(pb.at[s, y, :, tile[j]], dst.at[:, more_lanes(y, s)], o_recv.at[t])

    def cells(t, j, r=None):
        ref = whole[t]
        if r is None:
            two = [ref[:, :, :, tile[k]].reshape(ALL, TILE) for k in (j, 3 + j)]
        else:
            two = [ref[r, :, :, tile[k]].reshape(256, TILE) for k in (j, 3 + j)]
        return jnp.concatenate(two, axis=1)

    def turn(j):
        for q in range(4):
            turned[j, :, 256 * q : 256 * q + 256] = cells(0, j, q).T

    sub = lax.broadcasted_iota(jnp.int32, (1, 8, 256), 1)

    def fold_rows(s):
        v = (s[:, :8] + s[:, 8:]).reshape(2, 2, 4, 8, 256)
        a, b = v[:, 0].reshape(8, 8, 256), v[:, 1].reshape(8, 8, 256)
        low = sub < 4
        v = jnp.where(low, a, b) + pltpu.roll(jnp.where(low, b, a), 4, 1)
        for width in (2, 1):
            v = v.reshape(2, 2, width, 8, 256)
            a, b = v[:, 0].reshape(2 * width, 8, 256), v[:, 1].reshape(2 * width, 8, 256)
            v = jnp.where(
                lax.rem(sub, 2 * width) < width, a + pltpu.roll(a, 8 - width, 1), b + pltpu.roll(b, width, 1)
            )
        return v.reshape(CH, 256)

    def gram(t, j, const):
        @pl.loop(0, 4)
        def _(r):
            rows = pl.ds(pl.multiple_of(r * CH, CH), CH)
            left = cells(t, j, r)
            for q in range(4):
                cols = slice(256 * q, 256 * q + 256)
                s = jnp.dot(left, turned[j, :, cols], preferred_element_type=F32)
                s = s.reshape(CH, CH, 256) * consts[const][None]
                s = fold_rows(s)
                if j == 0:
                    acc[t, rows, cols] = s
                else:
                    acc[t, rows, cols] += s

    half = MEMBERS // 4
    own = pl.ds(pl.multiple_of(half * c, half), half)
    other = pl.ds(pl.multiple_of(half * (1 - c), half), half)

    def pack(t):
        rest = acc[t]
        parts = []
        for _ in range(3):
            parts.append(rest.astype(BF16))
            rest = rest - parts[-1].astype(F32)
        h = MEMBERS // 2
        low = jnp.concatenate([p[:h] for p in parts], axis=0)
        high = jnp.concatenate([p[h:] for p in parts], axis=0)
        both = jnp.dot(low, fold_lo[...], preferred_element_type=F32)
        both += jnp.dot(high, fold_hi[...], preferred_element_type=F32)
        packed[t] = both[:h] + both[h : 2 * h] + both[2 * h :]

    def swap(src, dst, send, recv, device):
        return pltpu.make_async_remote_copy(
            src_ref=src, dst_ref=dst, send_sem=send, recv_sem=recv, device_id=device, device_id_type=MESH
        )

    def run(copies):
        for copy in copies:
            copy.start()

    def collect(t, copies, src, buf, dst):
        for copy in copies:
            copy.wait()
        total = src[t]
        for i in range(len(copies)):
            total += buf[t, i]
        if dst is fin:
            fin[t, own] = total
        else:
            dst[t] = total

    def stage(t, name):
        if name == "core":
            return [swap(packed.at[t, other], cbuf.at[t], c_sem.at[t, 0], c_sem.at[t, 1], at(dc=1))]
        if name == "back":
            return [swap(fin.at[t, own], fin.at[t, own], f_sem.at[t, 0], f_sem.at[t, 1], at(dc=1))]
        if name == "plane":
            return [
                swap(ysrc.at[t], ybuf.at[t, i], y_sem.at[t, i, 0], y_sem.at[t, i, 1], at(dy=dy, dx=dx))
                for i, (dy, dx) in enumerate(PLANE)
            ]
        return [
            swap(zsrc.at[t], zbuf.at[t, d - 1], z_sem.at[t, d - 1, 0], z_sem.at[t, d - 1, 1], at(dz=d))
            for d in range(1, NZ)
        ]

    def reduce_begin(t, after_core, after_plane):
        pack(t)
        core = stage(t, "core")
        run(core)
        after_core()
        core[0].wait()
        ysrc[t] = packed[t, own] + cbuf[t]
        plane = stage(t, "plane")
        run(plane)
        after_plane()
        collect(t, plane, ysrc, ybuf, zsrc)
        run(stage(t, "z"))

    def reduce_z(t):
        collect(t, stage(t, "z"), zsrc, zbuf, fin)
        run(stage(t, "back"))

    def reduce_end(t):
        stage(t, "back")[0].wait()
        return jnp.concatenate([fin[t, :, :MEMBERS], fin[t, :, MEMBERS:]], axis=0)

    spread = (
        lax.broadcasted_iota(jnp.int32, (MEMBERS, ALL), 0)
        == lax.broadcasted_iota(jnp.int32, (MEMBERS, ALL), 1) // CH
    ).astype(BF16)

    def blocks(dst, *terms):
        @pl.loop(0, MEMBERS)
        def _(m):
            rows = pl.ds(pl.multiple_of(m * CH, CH), CH)
            for q in range(4):
                cols = slice(256 * q, 256 * q + 256)
                total = None
                for coefficient, const in terms:
                    term = jnp.broadcast_to(coefficient[pl.ds(m, 1), cols], (CH, 256)) * consts[const]
                    total = term if total is None else total + term
                dst[rows, cols] = total.astype(BF16)

    def put(t, j, r, value):
        value = value.astype(BF16)
        made[t][r, :, :, tile[j]] = value[:, :TILE].reshape(4, ROWS, TILE)
        made[t][r, :, :, tile[3 + j]] = value[:, TILE:].reshape(4, ROWS, TILE)

    barrier = pltpu.get_barrier_semaphore()
    partners = [at(dc=1)]
    partners += [at(dy=dy, dx=dx) for dy, dx in PLANE]
    partners += [at(dz=d) for d in range(1, NZ)]
    for device in partners:
        pl.semaphore_signal(barrier, inc=1, device_id=device, device_id_type=MESH)
    for i, ref in enumerate((wq_hbm, wk_hbm, wv_hbm, wo_hbm)):
        local(ref, weights_in.at[i], w_sem)
    pl.semaphore_wait(barrier, len(partners))

    for j in range(3):
        out1(0, j)
    local(e_hbm, e_out, k_sem.at[0])
    local(c_hbm, c_out, k_sem.at[1])

    @pl.when(jnp.logical_not(mine))
    def _():
        e_all[:, :, :, XLO:] = jnp.zeros((4, 4, ROWS, TILE), BF16)
        c_all[:, :, :, XLO:] = jnp.zeros((4, 4, ROWS, TILE), BF16)

    await_bytes(weights_in, w_sem)
    wq, wk, wv, wo = (weights_in[i] for i in range(4))
    a_mat = tn(wq, wk)
    at_mat = tn(wk, wq)
    m_mat = jnp.dot(wo, wv, preferred_element_type=F32)
    mt_mat = lax.dot_general(wv, wo, (((0,), (1,)), ((), ())), preferred_element_type=F32)
    row16 = lax.broadcasted_iota(jnp.int32, (CH, 256), 0)
    lane16 = lax.rem(lax.broadcasted_iota(jnp.int32, (CH, 256), 1), CH)
    repeat = (row16 == lane16).astype(F32)
    for i, mat in enumerate((a_mat, at_mat, m_mat, mt_mat)):
        consts[i] = jnp.dot(mat, repeat, precision=HIGH, preferred_element_type=F32)
    group = lax.broadcasted_iota(jnp.int32, (ALL, 2 * MEMBERS), 0) // CH
    column = lax.broadcasted_iota(jnp.int32, (ALL, 2 * MEMBERS), 1)
    fold_lo[...] = (group == column).astype(BF16)
    fold_hi[...] = (group == column - MEMBERS).astype(BF16)

    for j in range(3):
        out2(0, j)
    for j in range(3):
        arrived(0, j)
        if j < 2:
            out1(1, j)
        turn(j)
        gram(0, j, 0)

    def more_cotangent():
        out1(1, 2)
        out2(1, 0)

    reduce_begin(0, lambda: None, more_cotangent)
    out2(1, 1)
    out2(1, 2)
    reduce_z(0)
    arrived(1, 0)
    gram(1, 0, 2)
    scores = scale * reduce_end(0)
    exponent = jnp.exp(scores - jnp.max(scores, axis=1, keepdims=True))
    weights = exponent / jnp.sum(exponent, axis=1, keepdims=True)
    wsave[...] = weights
    w_half = weights.astype(BF16)
    exp_a[...] = jnp.dot(w_half, spread, preferred_element_type=F32)
    blocks(dmat, (exp_a, 2))

    def mix_branch(j):
        right = cells(0, j)
        for r in range(4):
            put(0, j, r, jnp.dot(dmat[256 * r : 256 * r + 256, :], right, preferred_element_type=F32))

    mix_branch(0)
    home1(0, 0)
    arrived(1, 1)
    gram(1, 1, 2)
    mix_branch(1)
    home1(0, 1)
    arrived(1, 2)
    gram(1, 2, 2)

    def more_branch():
        home2(0, 0)
        home1(0, 2)

    reduce_begin(1, lambda: mix_branch(2), more_branch)
    exp_b[...] = tn(wsave[...].astype(BF16), spread)
    blocks(tmat, (exp_b, 3))
    for j in range(3):
        right = cells(1, j)
        for r in range(4):
            rows = slice(256 * r, 256 * r + 256)
            partial[j, rows, :] = jnp.dot(tmat[rows, :], right, preferred_element_type=F32)
    home2(0, 1)
    reduce_z(1)
    home2(0, 2)
    pairs = reduce_end(1)
    weights = wsave[...]
    grad_scores = weights * (pairs - jnp.sum(weights * pairs, axis=1, keepdims=True))
    g_half = (scale * grad_scores).astype(BF16)
    exp_a[...] = jnp.dot(g_half, spread, preferred_element_type=F32)
    exp_b[...] = tn(g_half, spread)
    blocks(gmat, (exp_a, 0), (exp_b, 1))
    for j in range(3):
        right = cells(0, j)
        for r in range(4):
            rows = slice(256 * r, 256 * r + 256)
            out = jnp.dot(gmat[rows, :], right, preferred_element_type=F32)
            put(1, j, r, out + partial[j, rows, :])
        home1(1, j)
    for j in range(3):
        home2(1, j)

    await_bytes(e_out, k_sem.at[0])
    await_bytes(c_out, k_sem.at[1])
    for t in range(2):
        for sem in (s1_send, s2_send, q1_send, q2_send):
            await_bytes(ea1.at[pl.ds(0, 3)], sem.at[t, 0])
            await_bytes(ea1.at[pl.ds(0, 3), :, :, pl.ds(0, 2 * TILE)], sem.at[t, 1])

        @pl.when(mine)
        def _(t=t):
            await_bytes(ea1.at[pl.ds(0, 3), :, :, tile[2]], q1x_send.at[t])

        for d in HOPS:
            yd, xd = lax.rem(y + d, 4), lax.rem(x + d, 4)
            for k in range(4):

                @pl.when(has_more(yd, k))
                def _(t=t, d=d, k=k):
                    await_bytes(ea1.at[0, 0, :, tile[2]], s1x_send.at[t, d, k])

            @pl.when(has_more(y, xd))
            def _(t=t, d=d):
                await_bytes(ea1.at[0, :, :, tile[2]], s2x_send.at[t, d])

        for k in range(4):

            @pl.when(has_more(y, k))
            def _(t=t, k=k):
                await_bytes(ea1.at[0, pl.ds(0, 3), :, tile[2]], q2x_send.at[t, k])

        await_bytes(homes[t], o_recv.at[t])


def shards(scale, ensemble, cotangent, w_query, w_key, w_value, w_out):
    shape = ensemble.shape
    full = lambda: pltpu.VMEM((4, 4, ROWS, WIDTH), BF16)
    part = lambda: pltpu.VMEM((4, 4, ROWS, SPAN), BF16)
    square = lambda: pltpu.VMEM((ALL, ALL), BF16)
    small = lambda *lead: pltpu.VMEM((2,) + lead + (MEMBERS // 4, 2 * MEMBERS), F32)
    dma = pltpu.SemaphoreType.DMA
    flat = pltpu.VMEM((ROWS, CELL_DEV), BF16)
    vmem = pl.BlockSpec(memory_space=pltpu.VMEM)
    hbm = pl.BlockSpec(memory_space=pltpu.HBM)
    branch, grad, ens, cot = pl.pallas_call(
        functools.partial(kernel, scale),
        out_shape=(flat,) * 4,
        in_specs=[hbm] * 6,
        out_specs=(vmem,) * 4,
        scratch_shapes=[pltpu.VMEM((4, CH, CH), BF16)]
        + [part() for _ in range(4)]
        + [full() for _ in range(4)]
        + [part() for _ in range(4)]
        + [pltpu.VMEM((3, ALL, 2 * TILE), F32)]
        + [square() for _ in range(3)]
        + [
            pltpu.VMEM((3, 2 * TILE, ALL), BF16),
            pltpu.VMEM((2, MEMBERS, ALL), F32),
            pltpu.VMEM((4, CH, 256), F32),
            pltpu.VMEM((ALL, 2 * MEMBERS), BF16),
            pltpu.VMEM((ALL, 2 * MEMBERS), BF16),
            pltpu.VMEM((2, MEMBERS // 2, 2 * MEMBERS), F32),
            small(),
            small(),
            small(PEERS - 1),
            small(),
            small(NZ - 1),
            pltpu.VMEM((2, MEMBERS // 2, 2 * MEMBERS), F32),
            pltpu.VMEM((MEMBERS, MEMBERS), F32),
            pltpu.VMEM((MEMBERS, ALL), F32),
            pltpu.VMEM((MEMBERS, ALL), F32),
        ]
        + [
            dma,
            dma((2,)),
            dma((2, 2)),
            dma((2, 2, 3)),
            dma((2, 4, 4)),
            dma((2, 4)),
            dma((2, 2)),
            dma((2, 2, 3)),
            dma((2, 4)),
            dma((2,)),
            dma((2, 2)),
            dma((2, PEERS - 1, 2)),
            dma((2, NZ - 1, 2)),
            dma((2, 2)),
            dma((2, 2)),
            dma((2, 2, 3)),
            dma((2,)),
            dma((2, 4)),
            dma((2, 2)),
            dma((2, 4)),
            dma((2,)),
        ],
        compiler_params=pltpu.CompilerParams(
            collective_id=0, has_side_effects=True, vmem_limit_bytes=67043328 - 4 * ROWS * CELL_DEV * 2
        ),
    )(
        ensemble.reshape(ROWS, CELL_DEV),
        cotangent.reshape(ROWS, CELL_DEV),
        w_query,
        w_key,
        w_value,
        w_out,
    )
    updated = ens.reshape(shape).astype(F32) + branch.reshape(shape).astype(F32)
    ensemble_grad = cot.reshape(shape).astype(F32) + grad.reshape(shape).astype(F32)
    return updated, ensemble_grad


def solution(mesh):
    torus = Mesh(mesh.devices.reshape(NY, NX, NZ, NC), ("y", "x", "z", "c"))
    scale = 1.0 / (CELL_DEV * NZ * NC * math.sqrt(CH))
    placed = P(("y", "x"), None, ("z", "c"))
    return jax.shard_map(
        functools.partial(shards, scale),
        mesh=torus,
        in_specs=(placed, placed, P(), P(), P(), P()),
        out_specs=(placed, placed),
        check_vma=False,
    )
```

```python
import functools
import math

import jax
import jax.numpy as jnp
from jax import lax
from jax.experimental import pallas as pl
from jax.experimental.pallas import tpu as pltpu
from jax.sharding import Mesh
from jax.sharding import PartitionSpec as P

MESH = pl.DeviceIdType.MESH
F32 = jnp.float32
BF16 = jnp.bfloat16
HIGH = lax.Precision.HIGHEST

NX, NY, NZ, NC = 4, 4, 8, 2
PEERS = NX * NY
CH = 16
MEM_DEV = 4
ROWS = MEM_DEV * CH
MEMBERS = MEM_DEV * PEERS
ALL = ROWS * PEERS
TILE = 128
MAIN = 5
EXTRA = 10
WIDTH = (MAIN + 1) * TILE
CELL_DEV = 11520
SPAN = 3 * TILE
XLO = MAIN * TILE
HOPS = (1, 3, 2)
PLANE = [(dy, dx) for dy in HOPS + (0,) for dx in HOPS + (0,) if dy or dx]
PLANE.sort(key=lambda d: -(min(d[0], 4 - d[0]) + min(d[1], 4 - d[1])))


def tn(a, b, precision=None):
    return lax.dot_general(
        a, b, (((0,), (0,)), ((), ())), precision=precision, preferred_element_type=F32
    )


def kernel(
    scale,
    e_hbm,
    c_hbm,
    wq_hbm,
    wk_hbm,
    wv_hbm,
    wo_hbm,
    ob,
    og,
    e_out,
    c_out,
    weights_in,
    ea1,
    eb1,
    ca1,
    cb1,
    e_all,
    c_all,
    bm,
    gm,
    ba,
    bb,
    ga,
    gb,
    partial,
    dmat,
    tmat,
    gmat,
    turned,
    acc,
    consts,
    fold_lo,
    fold_hi,
    packed,
    cbuf,
    ysrc,
    ybuf,
    zsrc,
    zbuf,
    fin,
    wsave,
    exp_a,
    exp_b,
    w_sem,
    k_sem,
    s1_send,
    s1_recv,
    s1x_send,
    s1x_recv,
    s2_send,
    s2_recv,
    s2x_send,
    s2x_recv,
    c_sem,
    y_sem,
    z_sem,
    f_sem,
    q1_send,
    q1_recv,
    q1x_send,
    q1x_recv,
    q2_send,
    q2x_send,
    o_recv,
):
    y, x = lax.axis_index("y"), lax.axis_index("x")
    z, c = lax.axis_index("z"), lax.axis_index("c")
    sources = (e_hbm, c_hbm)
    first_a, first_b = (ea1, ca1), (eb1, cb1)
    whole = (e_all, c_all)
    made = (bm, gm)
    back_a, back_b = (ba, ga), (bb, gb)
    homes = (ob, og)

    def at(dy=0, dx=0, dz=0, dc=0):
        return (
            lax.rem(y + dy, NY),
            lax.rem(x + dx, NX),
            lax.rem(z + dz, NZ),
            lax.rem(c + dc, NC),
        )

    def more(yd, xd):
        return 4 * lax.rem(xd + yd, 4) + lax.rem(yd + 2 * c, 4)

    def has_more(yd, xd):
        return more(yd, xd) < EXTRA

    def lanes(yd, xd, lo):
        return pl.ds(pl.multiple_of((4 * yd + xd) * XLO + lo, TILE), TILE)

    def more_lanes(yd, xd):
        return pl.ds(pl.multiple_of((MAIN * PEERS + more(yd, xd)) * TILE, TILE), TILE)

    def remote(src, dst, send, recv, device):
        pltpu.make_async_remote_copy(
            src_ref=src, dst_ref=dst, send_sem=send, recv_sem=recv, device_id=device, device_id_type=MESH
        ).start()

    def local(src, dst, sem):
        pltpu.make_async_copy(src, dst, sem).start()

    def await_bytes(view, sem):
        pltpu.make_async_copy(view, view, sem).wait()

    mine = has_more(y, x)
    tile = [pl.ds(TILE * k, TILE) for k in range(6)]

    def out1(t, j):
        src, pa, pb = sources[t], first_a[t], first_b[t]
        for d in HOPS:

            @pl.loop(0, 4)
            def _(k, d=d):
                xd, yd = lax.rem(x + d, 4), lax.rem(y + d, 4)
                remote(
                    src.at[:, lanes(k, xd, TILE * j)],
                    pa.at[k, x, :, tile[j]],
                    s1_send.at[t, 0],
                    s1_recv.at[t, 0, j],
                    at(dx=d),
                )
                if j < 2:
                    remote(
                        src.at[:, lanes(yd, k, SPAN + TILE * j)],
                        pb.at[k, y, :, tile[j]],
                        s1_send.at[t, 1],
                        s1_recv.at[t, 1, j],
                        at(dy=d),
                    )
                else:

                    @pl.when(has_more(yd, k))
                    def _():
                        remote(
                            src.at[:, more_lanes(yd, k)],
                            pb.at[k, y, :, tile[j]],
                            s1x_send.at[t, d, k],
                            s1x_recv.at[t, k],
                            at(dy=d),
                        )

        @pl.loop(0, 4)
        def _(k):
            local(src.at[:, lanes(k, x, TILE * j)], pa.at[k, x, :, tile[j]], s1_recv.at[t, 0, j])
            if j < 2:
                local(src.at[:, lanes(y, k, SPAN + TILE * j)], pb.at[k, y, :, tile[j]], s1_recv.at[t, 1, j])
            else:

                @pl.when(has_more(y, k))
                def _():
                    local(src.at[:, more_lanes(y, k)], pb.at[k, y, :, tile[j]], s1x_recv.at[t, k])

    def out2(t, j):
        pa, pb, dst = first_a[t], first_b[t], whole[t]
        await_bytes(pa.at[:, :, :, tile[j]], s1_recv.at[t, 0, j])
        for d in HOPS:
            yd = lax.rem(y + d, 4)
            remote(
                pa.at[yd, :, :, tile[j]], dst.at[y, :, :, tile[j]], s2_send.at[t, 0], s2_recv.at[t, 0, j], at(dy=d)
            )
        local(pa.at[y, :, :, tile[j]], dst.at[y, :, :, tile[j]], s2_recv.at[t, 0, j])
        if j < 2:
            await_bytes(pb.at[:, :, :, tile[j]], s1_recv.at[t, 1, j])
            for d in HOPS:
                xd = lax.rem(x + d, 4)
                remote(
                    pb.at[xd, :, :, tile[j]],
                    dst.at[:, x, :, tile[3 + j]],
                    s2_send.at[t, 1],
                    s2_recv.at[t, 1, j],
                    at(dx=d),
                )
            local(pb.at[x, :, :, tile[j]], dst.at[:, x, :, tile[3 + j]], s2_recv.at[t, 1, j])
        else:
            for d in HOPS:
                xd = lax.rem(x + d, 4)

                @pl.when(has_more(y, xd))
                def _(d=d, xd=xd):
                    await_bytes(pb.at[xd, :, :, tile[j]], s1x_recv.at[t, xd])
                    remote(
                        pb.at[xd, :, :, tile[j]],
                        dst.at[:, x, :, tile[3 + j]],
                        s2x_send.at[t, d],
                        s2x_recv.at[t],
                        at(dx=d),
                    )

            @pl.when(mine)
            def _():
                await_bytes(pb.at[x, :, :, tile[j]], s1x_recv.at[t, x])
                local(pb.at[x, :, :, tile[j]], dst.at[:, x, :, tile[3 + j]], s2x_recv.at[t])

    def arrived(t, j):
        await_bytes(whole[t].at[:, :, :, tile[j]], s2_recv.at[t, 0, j])
        if j < 2:
            await_bytes(whole[t].at[:, :, :, tile[3 + j]], s2_recv.at[t, 1, j])
        else:

            @pl.when(mine)
            def _():
                await_bytes(whole[t].at[:, :, :, tile[3 + j]], s2x_recv.at[t])

    def home1(t, j):
        src, pa, pb = made[t], back_a[t], back_b[t]
        for d in HOPS:
            yh, xh = lax.rem(y + d, 4), lax.rem(x + d, 4)
            remote(
                src.at[yh, :, :, tile[j]], pa.at[y, :, :, tile[j]], q1_send.at[t, 0], q1_recv.at[t, 0, j], at(dy=d)
            )
            if j < 2:
                remote(
                    src.at[:, xh, :, tile[3 + j]],
                    pb.at[x, :, :, tile[j]],
                    q1_send.at[t, 1],
                    q1_recv.at[t, 1, j],
                    at(dx=d),
                )
        local(src.at[y, :, :, tile[j]], pa.at[y, :, :, tile[j]], q1_recv.at[t, 0, j])
        if j < 2:
            local(src.at[:, x, :, tile[3 + j]], pb.at[x, :, :, tile[j]], q1_recv.at[t, 1, j])
        else:

            @pl.when(mine)
            def _():
                for d in HOPS:
                    xh = lax.rem(x + d, 4)
                    remote(
                        src.at[:, xh, :, tile[3 + j]],
                        pb.at[x, :, :, tile[j]],
                        q1x_send.at[t],
                        q1x_recv.at[t, x],
                        at(dx=d),
                    )
                local(src.at[:, x, :, tile[3 + j]], pb.at[x, :, :, tile[j]], q1x_recv.at[t, x])

    def home2(t, j):
        pa, pb, dst = back_a[t], back_b[t], homes[t]
        await_bytes(pa.at[:, :, :, tile[j]], q1_recv.at[t, 0, j])

        @pl.loop(0, 4)
        def _(s):
            for d in HOPS:
                remote(
                    pa.at[s, lax.rem(x + d, 4), :, tile[j]],
                    dst.at[:, lanes(s, x, TILE * j)],
                    q2_send.at[t, 0],
                    o_recv.at[t],
                    at(dx=d),
                )
            local(pa.at[s, x, :, tile[j]], dst.at[:, lanes(s, x, TILE * j)], o_recv.at[t])

        if j < 2:
            await_bytes(pb.at[:, :, :, tile[j]], q1_recv.at[t, 1, j])

        @pl.loop(0, 4)
        def _(s):
            if j < 2:
                for d in HOPS:
                    remote(
                        pb.at[s, lax.rem(y + d, 4), :, tile[j]],
                        dst.at[:, lanes(y, s, SPAN + TILE * j)],
                        q2_send.at[t, 1],
                        o_recv.at[t],
                        at(dy=d),
                    )
                local(pb.at[s, y, :, tile[j]], dst.at[:, lanes(y, s, SPAN + TILE * j)], o_recv.at[t])
            else:

                @pl.when(has_more(y, s))
                def _():
                    await_bytes(pb.at[s, :, :, tile[j]], q1x_recv.at[t, s])
                    for d in HOPS:
                        remote(
                            pb.at[s, lax.rem(y + d, 4), :, tile[j]],
                            dst.at[:, more_lanes(y, s)],
                            q2x_send.at[t, s],
                            o_recv.at[t],
                            at(dy=d),
                        )
                    local(pb.at[s, y, :, tile[j]], dst.at[:, more_lanes(y, s)], o_recv.at[t])

    def cells(t, j, r=None):
        ref = whole[t]
        if r is None:
            two = [ref[:, :, :, tile[k]].reshape(ALL, TILE) for k in (j, 3 + j)]
        else:
            two = [ref[r, :, :, tile[k]].reshape(256, TILE) for k in (j, 3 + j)]
        return jnp.concatenate(two, axis=1)

    def turn(j):
        for q in range(4):
            turned[j, :, 256 * q : 256 * q + 256] = cells(0, j, q).T

    sub = lax.broadcasted_iota(jnp.int32, (1, 8, 256), 1)

    def fold_rows(s):
        v = (s[:, :8] + s[:, 8:]).reshape(2, 2, 4, 8, 256)
        a, b = v[:, 0].reshape(8, 8, 256), v[:, 1].reshape(8, 8, 256)
        low = sub < 4
        v = jnp.where(low, a, b) + pltpu.roll(jnp.where(low, b, a), 4, 1)
        for width in (2, 1):
            v = v.reshape(2, 2, width, 8, 256)
            a, b = v[:, 0].reshape(2 * width, 8, 256), v[:, 1].reshape(2 * width, 8, 256)
            v = jnp.where(
                lax.rem(sub, 2 * width) < width, a + pltpu.roll(a, 8 - width, 1), b + pltpu.roll(b, width, 1)
            )
        return v.reshape(CH, 256)

    def gram(t, j, const):
        @pl.loop(0, 4, unroll=2)
        def _(r):
            rows = pl.ds(pl.multiple_of(r * CH, CH), CH)
            left = cells(t, j, r)
            for q in range(4):
                cols = slice(256 * q, 256 * q + 256)
                s = jnp.dot(left, turned[j, :, cols], preferred_element_type=F32)
                s = s.reshape(CH, CH, 256) * consts[const][None]
                s = fold_rows(s)
                if j == 0:
                    acc[t, rows, cols] = s
                else:
                    acc[t, rows, cols] += s

    half = MEMBERS // 4
    own = pl.ds(pl.multiple_of(half * c, half), half)
    other = pl.ds(pl.multiple_of(half * (1 - c), half), half)

    def pack(t):
        rest = acc[t]
        parts = []
        for _ in range(3):
            parts.append(rest.astype(BF16))
            rest = rest - parts[-1].astype(F32)
        h = MEMBERS // 2
        low = jnp.concatenate([p[:h] for p in parts], axis=0)
        high = jnp.concatenate([p[h:] for p in parts], axis=0)
        both = jnp.dot(low, fold_lo[...], preferred_element_type=F32)
        both += jnp.dot(high, fold_hi[...], preferred_element_type=F32)
        packed[t] = both[:h] + both[h : 2 * h] + both[2 * h :]

    def swap(src, dst, send, recv, device):
        return pltpu.make_async_remote_copy(
            src_ref=src, dst_ref=dst, send_sem=send, recv_sem=recv, device_id=device, device_id_type=MESH
        )

    def run(copies):
        for copy in copies:
            copy.start()

    def collect(t, copies, src, buf, dst):
        for copy in copies:
            copy.wait()
        total = src[t]
        for i in range(len(copies)):
            total += buf[t, i]
        if dst is fin:
            fin[t, own] = total
        else:
            dst[t] = total

    def stage(t, name):
        if name == "core":
            return [swap(packed.at[t, other], cbuf.at[t], c_sem.at[t, 0], c_sem.at[t, 1], at(dc=1))]
        if name == "back":
            return [swap(fin.at[t, own], fin.at[t, own], f_sem.at[t, 0], f_sem.at[t, 1], at(dc=1))]
        if name == "plane":
            return [
                swap(ysrc.at[t], ybuf.at[t, i], y_sem.at[t, i, 0], y_sem.at[t, i, 1], at(dy=dy, dx=dx))
                for i, (dy, dx) in enumerate(PLANE)
            ]
        return [
            swap(zsrc.at[t], zbuf.at[t, d - 1], z_sem.at[t, d - 1, 0], z_sem.at[t, d - 1, 1], at(dz=d))
            for d in range(1, NZ)
        ]

    def reduce_begin(t, after_core, after_plane):
        pack(t)
        core = stage(t, "core")
        run(core)
        after_core()
        core[0].wait()
        ysrc[t] = packed[t, own] + cbuf[t]
        plane = stage(t, "plane")
        run(plane)
        after_plane()
        collect(t, plane, ysrc, ybuf, zsrc)
        run(stage(t, "z"))

    def reduce_z(t):
        collect(t, stage(t, "z"), zsrc, zbuf, fin)
        run(stage(t, "back"))

    def reduce_end(t):
        stage(t, "back")[0].wait()
        return jnp.concatenate([fin[t, :, :MEMBERS], fin[t, :, MEMBERS:]], axis=0)

    spread = (
        lax.broadcasted_iota(jnp.int32, (MEMBERS, ALL), 0)
        == lax.broadcasted_iota(jnp.int32, (MEMBERS, ALL), 1) // CH
    ).astype(BF16)

    def blocks(dst, *terms):
        @pl.loop(0, MEMBERS, unroll=4)
        def _(m):
            rows = pl.ds(pl.multiple_of(m * CH, CH), CH)
            for q in range(4):
                cols = slice(256 * q, 256 * q + 256)
                total = None
                for coefficient, const in terms:
                    term = jnp.broadcast_to(coefficient[pl.ds(m, 1), cols], (CH, 256)) * consts[const]
                    total = term if total is None else total + term
                dst[rows, cols] = total.astype(BF16)

    def put(t, j, r, value):
        value = value.astype(BF16)
        made[t][r, :, :, tile[j]] = value[:, :TILE].reshape(4, ROWS, TILE)
        made[t][r, :, :, tile[3 + j]] = value[:, TILE:].reshape(4, ROWS, TILE)

    barrier = pltpu.get_barrier_semaphore()
    partners = [at(dc=1)]
    partners += [at(dy=dy, dx=dx) for dy, dx in PLANE]
    partners += [at(dz=d) for d in range(1, NZ)]
    for device in partners:
        pl.semaphore_signal(barrier, inc=1, device_id=device, device_id_type=MESH)
    for i, ref in enumerate((wq_hbm, wk_hbm, wv_hbm, wo_hbm)):
        local(ref, weights_in.at[i], w_sem)
    pl.semaphore_wait(barrier, len(partners))

    for j in range(3):
        out1(0, j)
    local(e_hbm, e_out, k_sem.at[0])
    local(c_hbm, c_out, k_sem.at[1])

    @pl.when(jnp.logical_not(mine))
    def _():
        e_all[:, :, :, XLO:] = jnp.zeros((4, 4, ROWS, TILE), BF16)
        c_all[:, :, :, XLO:] = jnp.zeros((4, 4, ROWS, TILE), BF16)

    await_bytes(weights_in, w_sem)
    wq, wk, wv, wo = (weights_in[i] for i in range(4))
    a_mat = tn(wq, wk)
    at_mat = tn(wk, wq)
    m_mat = jnp.dot(wo, wv, preferred_element_type=F32)
    mt_mat = lax.dot_general(wv, wo, (((0,), (1,)), ((), ())), preferred_element_type=F32)
    row16 = lax.broadcasted_iota(jnp.int32, (CH, 256), 0)
    lane16 = lax.rem(lax.broadcasted_iota(jnp.int32, (CH, 256), 1), CH)
    repeat = (row16 == lane16).astype(F32)
    for i, mat in enumerate((a_mat, at_mat, m_mat, mt_mat)):
        consts[i] = jnp.dot(mat, repeat, precision=HIGH, preferred_element_type=F32)
    group = lax.broadcasted_iota(jnp.int32, (ALL, 2 * MEMBERS), 0) // CH
    column = lax.broadcasted_iota(jnp.int32, (ALL, 2 * MEMBERS), 1)
    fold_lo[...] = (group == column).astype(BF16)
    fold_hi[...] = (group == column - MEMBERS).astype(BF16)

    for j in range(3):
        out2(0, j)
    for j in range(3):
        arrived(0, j)
        if j < 2:
            out1(1, j)
        turn(j)
        gram(0, j, 0)

    def more_cotangent():
        out1(1, 2)
        out2(1, 0)

    reduce_begin(0, lambda: None, more_cotangent)
    out2(1, 1)
    out2(1, 2)
    reduce_z(0)
    arrived(1, 0)
    gram(1, 0, 2)
    scores = scale * reduce_end(0)
    exponent = jnp.exp(scores - jnp.max(scores, axis=1, keepdims=True))
    weights = exponent / jnp.sum(exponent, axis=1, keepdims=True)
    wsave[...] = weights
    w_half = weights.astype(BF16)
    exp_a[...] = jnp.dot(w_half, spread, preferred_element_type=F32)
    blocks(dmat, (exp_a, 2))

    def mix_branch(j):
        right = cells(0, j)
        for r in range(4):
            put(0, j, r, jnp.dot(dmat[256 * r : 256 * r + 256, :], right, preferred_element_type=F32))

    mix_branch(0)
    home1(0, 0)
    arrived(1, 1)
    gram(1, 1, 2)
    mix_branch(1)
    home1(0, 1)
    arrived(1, 2)
    gram(1, 2, 2)

    def more_branch():
        home2(0, 0)
        home1(0, 2)

    reduce_begin(1, lambda: mix_branch(2), more_branch)
    exp_b[...] = tn(wsave[...].astype(BF16), spread)
    blocks(tmat, (exp_b, 3))
    for j in range(3):
        right = cells(1, j)
        for r in range(4):
            rows = slice(256 * r, 256 * r + 256)
            partial[j, rows, :] = jnp.dot(tmat[rows, :], right, preferred_element_type=F32)
    home2(0, 1)
    reduce_z(1)
    home2(0, 2)
    pairs = reduce_end(1)
    weights = wsave[...]
    grad_scores = weights * (pairs - jnp.sum(weights * pairs, axis=1, keepdims=True))
    g_half = (scale * grad_scores).astype(BF16)
    exp_a[...] = jnp.dot(g_half, spread, preferred_element_type=F32)
    exp_b[...] = tn(g_half, spread)
    blocks(gmat, (exp_a, 0), (exp_b, 1))
    for j in range(3):
        right = cells(0, j)
        for r in range(4):
            rows = slice(256 * r, 256 * r + 256)
            out = jnp.dot(gmat[rows, :], right, preferred_element_type=F32)
            put(1, j, r, out + partial[j, rows, :])
        home1(1, j)
    for j in range(3):
        home2(1, j)

    await_bytes(e_out, k_sem.at[0])
    await_bytes(c_out, k_sem.at[1])
    for t in range(2):
        for sem in (s1_send, s2_send, q1_send, q2_send):
            await_bytes(ea1.at[pl.ds(0, 3)], sem.at[t, 0])
            await_bytes(ea1.at[pl.ds(0, 3), :, :, pl.ds(0, 2 * TILE)], sem.at[t, 1])

        @pl.when(mine)
        def _(t=t):
            await_bytes(ea1.at[pl.ds(0, 3), :, :, tile[2]], q1x_send.at[t])

        for d in HOPS:
            yd, xd = lax.rem(y + d, 4), lax.rem(x + d, 4)
            for k in range(4):

                @pl.when(has_more(yd, k))
                def _(t=t, d=d, k=k):
                    await_bytes(ea1.at[0, 0, :, tile[2]], s1x_send.at[t, d, k])

            @pl.when(has_more(y, xd))
            def _(t=t, d=d):
                await_bytes(ea1.at[0, :, :, tile[2]], s2x_send.at[t, d])

        for k in range(4):

            @pl.when(has_more(y, k))
            def _(t=t, k=k):
                await_bytes(ea1.at[0, pl.ds(0, 3), :, tile[2]], q2x_send.at[t, k])

        await_bytes(homes[t], o_recv.at[t])


def shards(scale, ensemble, cotangent, w_query, w_key, w_value, w_out):
    shape = ensemble.shape
    full = lambda: pltpu.VMEM((4, 4, ROWS, WIDTH), BF16)
    part = lambda: pltpu.VMEM((4, 4, ROWS, SPAN), BF16)
    square = lambda: pltpu.VMEM((ALL, ALL), BF16)
    small = lambda *lead: pltpu.VMEM((2,) + lead + (MEMBERS // 4, 2 * MEMBERS), F32)
    dma = pltpu.SemaphoreType.DMA
    flat = pltpu.VMEM((ROWS, CELL_DEV), BF16)
    vmem = pl.BlockSpec(memory_space=pltpu.VMEM)
    hbm = pl.BlockSpec(memory_space=pltpu.HBM)
    branch, grad, ens, cot = pl.pallas_call(
        functools.partial(kernel, scale),
        out_shape=(flat,) * 4,
        in_specs=[hbm] * 6,
        out_specs=(vmem,) * 4,
        scratch_shapes=[pltpu.VMEM((4, CH, CH), BF16)]
        + [part() for _ in range(4)]
        + [full() for _ in range(4)]
        + [part() for _ in range(4)]
        + [pltpu.VMEM((3, ALL, 2 * TILE), F32)]
        + [square() for _ in range(3)]
        + [
            pltpu.VMEM((3, 2 * TILE, ALL), BF16),
            pltpu.VMEM((2, MEMBERS, ALL), F32),
            pltpu.VMEM((4, CH, 256), F32),
            pltpu.VMEM((ALL, 2 * MEMBERS), BF16),
            pltpu.VMEM((ALL, 2 * MEMBERS), BF16),
            pltpu.VMEM((2, MEMBERS // 2, 2 * MEMBERS), F32),
            small(),
            small(),
            small(PEERS - 1),
            small(),
            small(NZ - 1),
            pltpu.VMEM((2, MEMBERS // 2, 2 * MEMBERS), F32),
            pltpu.VMEM((MEMBERS, MEMBERS), F32),
            pltpu.VMEM((MEMBERS, ALL), F32),
            pltpu.VMEM((MEMBERS, ALL), F32),
        ]
        + [
            dma,
            dma((2,)),
            dma((2, 2)),
            dma((2, 2, 3)),
            dma((2, 4, 4)),
            dma((2, 4)),
            dma((2, 2)),
            dma((2, 2, 3)),
            dma((2, 4)),
            dma((2,)),
            dma((2, 2)),
            dma((2, PEERS - 1, 2)),
            dma((2, NZ - 1, 2)),
            dma((2, 2)),
            dma((2, 2)),
            dma((2, 2, 3)),
            dma((2,)),
            dma((2, 4)),
            dma((2, 2)),
            dma((2, 4)),
            dma((2,)),
        ],
        compiler_params=pltpu.CompilerParams(
            collective_id=0, has_side_effects=True, vmem_limit_bytes=67043328 - 4 * ROWS * CELL_DEV * 2
        ),
    )(
        ensemble.reshape(ROWS, CELL_DEV),
        cotangent.reshape(ROWS, CELL_DEV),
        w_query,
        w_key,
        w_value,
        w_out,
    )
    updated = ens.reshape(shape).astype(F32) + branch.reshape(shape).astype(F32)
    ensemble_grad = cot.reshape(shape).astype(F32) + grad.reshape(shape).astype(F32)
    return updated, ensemble_grad


def solution(mesh):
    torus = Mesh(mesh.devices.reshape(NY, NX, NZ, NC), ("y", "x", "z", "c"))
    scale = 1.0 / (CELL_DEV * NZ * NC * math.sqrt(CH))
    placed = P(("y", "x"), None, ("z", "c"))
    return jax.shard_map(
        functools.partial(shards, scale),
        mesh=torus,
        in_specs=(placed, placed, P(), P(), P(), P()),
        out_specs=(placed, placed),
        check_vma=False,
    )
```
